32 devices in a mesh: groups: 2 (over x), views: 16 (over z, y, core).
Axes of the slice: x: 2, y: 2, z: 4, core: 2. Of those that a mesh axis runs over, the one named last changes fastest.
Arguments:
- source_rows: bfloat16 [384, 320, 128], P(('groups', 'views')), parts along dimension 0, may hold values from -6 to 6
- route_owner: int32 [384, 1], P(('groups', 'views')), parts along dimension 0, may hold values from 0 to 15; in each aligned block of 12 rows (0 to 11, 12 to 23, ...) at most 2 rows name the same one
- target_row: int32 [384], P(('groups', 'views')), parts along dimension 0, may hold values from 0 to 3
- start_index: int32 [384], P(('groups', 'views')), parts along dimension 0, may hold values from 0 to 15
- reference_rows: bfloat16 [128, 320, 128], P(('groups', 'views')), parts along dimension 0, may hold values from -96 to 96
- conv_weight: float32 [40, 3, 3, 3], replicated, may hold values from -3 to 3
Outputs:
- depth_map: float32 [128, 128], P(('groups', 'views')), parts along dimension 0
The draws below stay inside these ranges and needn't reach their ends.
There are 2 independent parts, one for each index of `groups`. The reference program is written for one: setup_inputs(seed, part) draws one part's arguments, and reference() takes and returns one part's arrays. A program takes and returns all parts, laid end to end along the dimension named above; an argument that names none is the same for every part. Nothing has to cross between parts.
Inputs may be any that keep to these rules, and one draw needn't show every extreme that they name: `route_owner`: among the rows of one device, no owner is named more than 2 times, a bound that some block reaches.
All inputs are finite; a program needn't handle non-finite values.
Results may differ from the reference program's by a relative error of at most 0.0003.
Values may be sent and summed in bfloat16 or wider, within the bound.
No kernel may reach another device: no remote copies, remote signals or barrier semaphores. Data moves between devices by JAX's collectives and lax.ppermute only.
A program may use at most 128 MiB of HBM per device.

```python
import math
import jax
import jax.numpy as jnp
import numpy as np
from jax import lax

C = 320
G = 40
CG = 8
DISP = 96
TW = 128
DSPAN = 16
CAP = 2
RR = 4
ITEMS = 12
SOURCES = 192
ROWS_ALL = 64
N_VIEWS = 16


def draw_reference_rows(key, part):
    values = jax.random.normal(key, (ROWS_ALL, C, TW), jnp.float32)
    values = jnp.clip(values, -6.0, 6.0)
    return values.astype(jnp.bfloat16)


def set_ends(values, stream_key, smallest, high):
    spot = [jax.random.randint(jax.random.fold_in(stream_key, axis), (), 0, length) for axis, length in enumerate(values.shape)]
    widest = values.shape.index(max(values.shape))
    neighbour = spot[:widest] + [(spot[widest] + 1) % values.shape[widest]] + spot[widest + 1:]
    return values.at[tuple(spot)].set(smallest).at[tuple(neighbour)].set(high)


def block_scale(rng, extent, split, least, top_value):
    factor_of, own = 1.0, jax.random.fold_in(rng, 6)
    for axis_at, shards_of in split:
        draws = jnp.exp(jax.random.uniform(jax.random.fold_in(own, axis_at), (shards_of,), jnp.float32, least / len(split), top_value / len(split)))
        factor_of = factor_of * jnp.repeat(draws, extent[axis_at] // shards_of).reshape([-1 if axis == axis_at else 1 for axis in range(len(extent))])
    return factor_of


def assign_block(rng, own, number, rows, count, top, bound, slope):
    order = jax.random.permutation(rng, count)
    crowded, ordinary = shares(count, rows * top, bound, slope, True), shares(count, rows * top, bound, slope, False)
    places = jnp.arange(count)

    def named(lengths, rotation):
        used = int((lengths > 0).sum())
        fixed = max(1, used // 4)
        passed = fixed + (places - fixed + rotation * (used - fixed)) % max(1, count - fixed)
        return jnp.zeros((count,), jnp.int32).at[order[jnp.where(places < fixed, places, passed)]].set(jnp.asarray(lengths, jnp.int32))

    lengths = jnp.where(number % 4 == 0, named(crowded, number // 4), named(ordinary, number - number // 4 - 1))
    mixed = jax.random.permutation(jax.random.fold_in(own, 3), count)
    donor, taker = mixed[0:count // 2 * 2:2], mixed[1:count // 2 * 2:2]
    slack = jnp.minimum(lengths[donor] - 1, bound - lengths[taker]) // 2
    slack = jnp.where((donor == order[0]) | (taker == order[0]) | (lengths[taker] == 0), 0, jnp.maximum(slack, 0))
    passed = jax.random.randint(jax.random.fold_in(own, 4), (count // 2,), 0, 1 << 20) % (slack + 1)
    lengths = lengths.at[donor].add(-passed).at[taker].add(passed)
    items = jnp.searchsorted(jnp.cumsum(lengths), jnp.arange(rows * top), side="right").astype(jnp.int32)
    table = items.reshape(top, rows).T
    table = table[jax.random.permutation(jax.random.fold_in(own, 1), rows)]
    rotation = jax.random.randint(jax.random.fold_in(own, 2), (rows, 1), 0, top)
    return jnp.take_along_axis(table, (jnp.arange(top)[None, :] + rotation) % top, axis=1)


def shares(count, total, limit, skew, full):
    weights = [(1 << 20) // math.isqrt(grade ** skew) + 1 for grade in range(1, count + 1)]
    largest = limit if full else min(limit, max(-(-total // count), total * weights[0] // sum(weights)))
    least = 1 if total - largest >= count - 1 else 0
    counts, surplus = [largest] + [least] * (count - 1), total - largest - least * (count - 1)
    while surplus > 0:
        candidates = [i for i in range(1, count) if counts[i] < largest] or [i for i in range(1, count) if counts[i] < limit]
        pool, remaining = sum([weights[i] for i in candidates]), surplus
        for i in candidates:
            more = min(limit - counts[i], max(1, remaining * weights[i] // pool), surplus)
            counts[i] = counts[i] + more
            surplus = surplus - more
    return np.array(counts)


def noise(key, extent, width, limit, shards=(), held_as=jnp.bfloat16):
    gain = block_scale(key, extent, shards, -0.22, 0.18) if shards else 1.0
    result = jax.random.normal(key, extent, jnp.float32) * width * gain
    return jnp.minimum(jnp.maximum(result, -limit), limit).astype(held_as)


def setup_inputs(seed: int = 0, part: int = 0) -> dict:
    arg_keys = jax.random.split(jax.random.key(seed), 7)
    part_keys = jax.random.split(jax.random.fold_in(arg_keys[6], part), 7)
    source_rows = noise(part_keys[0], (SOURCES, C, TW), 1.0, 6.0, ((0, 16),))
    route_owner_keys = jax.random.split(jax.random.fold_in(part_keys[1], 1), SOURCES // ITEMS)
    route_owner_turns = jax.random.permutation(jax.random.fold_in(part_keys[1], 3), SOURCES // ITEMS)
    route_owner = jax.vmap(lambda own, number: assign_block(jax.random.fold_in(part_keys[1], 2), own, number, ITEMS, N_VIEWS, 1, CAP, 2))(route_owner_keys, route_owner_turns).reshape((SOURCES, 1))
    target_row = set_ends(jax.random.randint(part_keys[2], (SOURCES,), 0, RR), jax.random.fold_in(part_keys[2], 1), 0, RR - 1).astype(jnp.int32)
    start_index = set_ends(jax.random.randint(part_keys[3], (SOURCES,), 0, DSPAN), jax.random.fold_in(part_keys[3], 1), 0, DSPAN - 1).astype(jnp.int32)
    reference_rows = draw_reference_rows(jax.random.fold_in(jax.random.fold_in(arg_keys[6], part), 71), part)
    conv_weight = noise(arg_keys[5], (G, 3, 3, 3), 0.5, 3.0, (), jnp.float32)
    return dict(source_rows=source_rows, route_owner=route_owner, target_row=target_row, start_index=start_index, reference_rows=reference_rows, conv_weight=conv_weight)


def make_canvas(feature, start_value):
    widened = jnp.pad(feature.astype(jnp.float32), ((0, 0), (DISP + DSPAN - 2, TW - DISP + 1)))
    offset = (DSPAN - 1 - start_value).astype(jnp.int32)
    return lax.dynamic_slice_in_dim(widened, offset, 2 * TW, 1)


def reference(source_rows, route_owner, target_row, start_index, reference_rows, conv_weight):
    owner_row = (route_owner[:, 0] * RR + target_row).astype(jnp.int32)

    def add_item(running_sum, item_entry):
        feature, row_index, start_value = item_entry
        canvas = make_canvas(feature, start_value)
        previous = lax.dynamic_slice_in_dim(running_sum, row_index, 1, 0)
        running_sum = lax.dynamic_update_slice_in_dim(running_sum, previous + canvas[None], row_index, 0)
        return running_sum, None

    summed = jnp.zeros((ROWS_ALL, C, 2 * TW), jnp.float32)
    summed, _ = lax.scan(add_item, summed, (source_rows, owner_row, start_index))
    pair_count = jax.ops.segment_sum(jnp.ones((SOURCES,), jnp.float32), owner_row, num_segments=ROWS_ALL)
    mean_canvas = summed / jnp.maximum(pair_count, 1.0)[:, None, None]
    mean_padded = jnp.pad(mean_canvas, ((1, 1), (0, 0), (0, 0)))
    reference_padded = jnp.pad(reference_rows.astype(jnp.float32), ((1, 1), (0, 0), (0, 0)))
    columns = jnp.arange(TW, dtype=jnp.int32)[None, :] + (DISP - 1) - jnp.arange(DISP, dtype=jnp.int32)[:, None]
    kernel_table = conv_weight.reshape(G, 27)
    levels = jnp.arange(DISP, dtype=jnp.float32) / DISP

    def one_band(band_index):
        first_row = (band_index * RR).astype(jnp.int32)
        reference_part = lax.dynamic_slice_in_dim(reference_padded, first_row, RR + 2, 0)
        canvas_part = lax.dynamic_slice_in_dim(mean_padded, first_row, RR + 2, 0)
        window = canvas_part[:, :, columns]
        product = reference_part[:, :, None, :] * window
        volume = jnp.sum(product.reshape(RR + 2, G, CG, DISP, TW), axis=2) / CG
        padded = jnp.pad(volume, ((0, 0), (0, 0), (1, 1), (1, 1)))
        taps_all = jnp.einsum('rgkx,gt->trkx', padded, kernel_table, precision=lax.Precision.HIGHEST)
        scores = jnp.zeros((RR, DISP, TW), jnp.float32)
        for shift_row in range(3):
            for shift_level in range(3):
                for shift_pixel in range(3):
                    tap_index = 9 * shift_row + 3 * shift_level + shift_pixel
                    scores = scores + taps_all[tap_index, shift_row:shift_row + RR, shift_level:shift_level + DISP, shift_pixel:shift_pixel + TW]
        weights = jax.nn.softmax(scores, axis=1)
        return jnp.sum(weights * levels[None, :, None], axis=1)

    bands = lax.map(one_band, jnp.arange(N_VIEWS, dtype=jnp.int32))
    return bands.reshape(ROWS_ALL, TW)
```

```python
import functools

import jax
import jax.numpy as jnp
from jax import lax
from jax.experimental import pallas as pl
from jax.experimental.pallas import tpu as pltpu
from jax.sharding import PartitionSpec as P

CG = 8
DISP = 96
DSPAN = 16
CAP = 2
CHUNKS = 4

VMEM = pl.BlockSpec(memory_space=pltpu.VMEM)
SMEM = pl.BlockSpec(memory_space=pltpu.SMEM)
ANY = pl.BlockSpec(memory_space=pl.ANY)


def pack_kernel(parts, route_ref, target_ref, start_ref, source_ref, *rest):
    outs, meta_ref, count_ref, sem = rest[:parts], rest[parts], rest[parts + 1], rest[parts + 2]
    items, channels = source_ref.shape[0], source_ref.shape[1]
    slots = meta_ref.shape[0]
    width = channels // parts

    @pl.loop(0, slots)
    def _(s):
        meta_ref[s] = -1

    @pl.loop(0, slots // CAP)
    def _(s):
        count_ref[s] = 0

    @pl.loop(0, items)
    def _(i):
        owner = route_ref[i, 0]
        slot = owner * CAP + count_ref[owner]
        count_ref[owner] = count_ref[owner] + 1
        meta_ref[slot] = target_ref[i] * DSPAN + start_ref[i]
        for p in range(parts):
            pltpu.make_async_copy(
                source_ref.at[i, pl.ds(p * width, width), :], outs[p].at[slot], sem
            ).start()

    @pl.loop(0, items)
    def _(i):
        for p in range(parts):
            pltpu.make_async_copy(
                source_ref.at[0, pl.ds(p * width, width), :], outs[p].at[0], sem
            ).wait()


def pack_rows(route, target, start, source, slots, parts):
    items, channels, pixels = source.shape
    width = channels // parts
    return pl.pallas_call(
        functools.partial(pack_kernel, parts),
        out_shape=[jax.ShapeDtypeStruct((slots, width, pixels), source.dtype)] * parts
        + [jax.ShapeDtypeStruct((slots,), jnp.int32)],
        in_specs=[SMEM, SMEM, SMEM, VMEM],
        out_specs=[ANY] * parts + [SMEM],
        scratch_shapes=[pltpu.SMEM((slots // CAP,), jnp.int32), pltpu.SemaphoreType.DMA],
        name="pack_rows",
    )(route, target, start, source)


def split_two(values):
    high = values.astype(jnp.bfloat16)
    return high, (values - high.astype(jnp.float32)).astype(jnp.bfloat16)


def shift_left(values, offset):
    lane = lax.broadcasted_iota(jnp.int32, values.shape, 1)
    pixels = values.shape[1]
    moved = pltpu.roll(values, (-offset) % pixels, 1)
    return jnp.where((lane + offset >= 0) & (lane + offset < pixels), moved, 0.0)


def chunk_kernel(first, last, meta_ref, arrived_ref, left_ref, weight_ref, edge_ref, *rest):
    if first:
        total_ref, canvas_ref = rest
        total_ref[...] = jnp.zeros_like(total_ref)
    elif last:
        before_ref, out_ref, canvas_ref, total_ref = rest
        total_ref[...] = before_ref[...]
    else:
        before_ref, total_ref, canvas_ref = rest
        total_ref[...] = before_ref[...]
    slots, width, pixels = arrived_ref.shape
    rows = canvas_ref.shape[0]
    canvas_ref[...] = jnp.zeros_like(canvas_ref)
    lane = lax.broadcasted_iota(jnp.int32, (width, pixels), 1)

    def add_slot(s, counts):
        code = meta_ref[s]
        row = code // DSPAN
        begin = code % DSPAN

        @pl.when(code >= 0)
        def _():
            moved = pltpu.roll(arrived_ref[s].astype(jnp.float32), begin, 1)
            canvas_ref[row] = canvas_ref[row] + jnp.where(lane >= begin, moved, 0.0)

        return tuple(
            count + jnp.where((code >= 0) & (row == r), 1, 0) for r, count in enumerate(counts)
        )

    counts = lax.fori_loop(0, slots, add_slot, (jnp.int32(0),) * rows)

    @pl.loop(0, rows)
    def _(r):
        count = counts[0]
        for other in range(1, rows):
            count = jnp.where(r == other, counts[other], count)
        mean = canvas_ref[r] / jnp.full(
            (width, pixels), jnp.maximum(count, 1).astype(jnp.float32)
        )
        right = jnp.concatenate([shift_left(mean, e) for e in (-1, 0, 1)], axis=0)
        high, low = split_two(right)
        both = jnp.concatenate([high, low], axis=1)
        edge = jnp.broadcast_to(mean[:, :1], (width, pixels)) * edge_ref[...]
        blank = jnp.zeros((2 * width, pixels), jnp.float32)
        edge_high, edge_low = split_two(jnp.concatenate([blank, edge], axis=0))
        wide = jnp.dot(
            left_ref[r],
            jnp.concatenate([edge_high, edge_low], axis=1),
            preferred_element_type=jnp.float32,
        )
        place = (rows + 2) * 3 + r
        total_ref[place] = total_ref[place] + (wide[:, :pixels] + wide[:, pixels:])
        left = left_ref[r].astype(jnp.float32)
        for a in range(3):
            for b in range(3):
                tap = 3 * a + b
                left_high, left_low = split_two(left * weight_ref[tap : tap + 1, :])
                wide = jnp.dot(left_high, both, preferred_element_type=jnp.float32)
                part = wide[:, :pixels] + wide[:, pixels:]
                part = part + jnp.dot(left_low, high, preferred_element_type=jnp.float32)
                place = (r + 2 - a) * 3 + b
                total_ref[place] = total_ref[place] + part

    if last:
        x = lax.broadcasted_iota(jnp.int32, (pixels, pixels), 0)
        v = lax.broadcasted_iota(jnp.int32, (pixels, pixels), 1)
        inside = (x >= v) & (x - v < DISP)

        @pl.loop(0, rows + 2)
        def _(r):
            total = jnp.where(inside, total_ref[3 * r + 1], 0.0)
            for b in (0, 2):
                kept = jnp.where(inside, total_ref[3 * r + b], 0.0)
                total = total + pltpu.roll(kept, (b - 1) % pixels, 1)
            out_ref[r] = total

        border = (x < DISP - 1) & ((v >= pixels - 2) | (v < 1))
        for r in range(rows):
            edge = total_ref[(rows + 2) * 3 + r]
            for a in range(3):
                moved = pltpu.roll(edge, (-8 * a) % pixels, 1) if a else edge
                out_ref[r + 2 - a] = out_ref[r + 2 - a] + jnp.where(border, moved, 0.0)


def add_chunk(first, last, meta, arrived, left, weight, edge, before):
    slots, width, pixels = arrived.shape
    rows = left.shape[0]
    totals = ((rows + 2) * 3 + rows, pixels, pixels)
    args = [meta, arrived, left, weight, edge] + ([] if first else [before])
    shape = (rows + 2, pixels, pixels) if last else totals
    scratch = [pltpu.VMEM((rows, width, pixels), jnp.float32)]
    if last:
        scratch.append(pltpu.VMEM(totals, jnp.float32))
    flops = 2 * rows * 27 * pixels * pixels * 3 * width
    return pl.pallas_call(
        functools.partial(chunk_kernel, first, last),
        out_shape=jax.ShapeDtypeStruct(shape, jnp.float32),
        in_specs=[SMEM] + [VMEM] * (len(args) - 1),
        out_specs=VMEM,
        scratch_shapes=scratch,
        cost_estimate=pl.CostEstimate(
            flops=flops,
            bytes_accessed=2 * slots * width * pixels + 8 * totals[0] * pixels * pixels,
            transcendentals=0,
        ),
        name="add_chunk",
    )(*args)


def depth_kernel(scores_ref, before_ref, after_ref, out_ref):
    rows = out_ref.shape[0]
    pixels = out_ref.shape[1]
    v = lax.broadcasted_iota(jnp.int32, (pixels, pixels), 0)
    x = lax.broadcasted_iota(jnp.int32, (pixels, pixels), 1)
    level = jnp.where(x >= v, x - v, x - v + pixels)
    valid = level < DISP
    share = level.astype(jnp.float32) / DISP
    for r in range(rows):
        scores = scores_ref[r + 1]
        if r == 0:
            scores = scores + before_ref[0]
        if r == rows - 1:
            scores = scores + after_ref[0]
        scores = jnp.where(valid, scores.T, -jnp.inf)
        top = jnp.max(scores, axis=0, keepdims=True)
        weights = jnp.exp(scores - top)
        bottom = jnp.sum(weights, axis=0, keepdims=True)
        out_ref[r : r + 1, :] = jnp.sum(weights * share, axis=0, keepdims=True) / bottom


def depth_rows(scores, before, after):
    rows, pixels = scores.shape[0] - 2, scores.shape[1]
    return pl.pallas_call(
        depth_kernel,
        out_shape=jax.ShapeDtypeStruct((rows, pixels), jnp.float32),
        in_specs=[VMEM] * 3,
        out_specs=VMEM,
        name="depth_rows",
    )(scores, before, after)


def body(source_rows, route_owner, target_row, start_index, reference_rows, conv_weight):
    owners = lax.axis_size("views")
    slots = owners * CAP
    rows, channels, pixels = reference_rows.shape
    parts = CHUNKS
    width = channels // parts
    packed = pack_rows(route_owner, target_row, start_index, source_rows, slots, parts)
    swap = functools.partial(
        lax.all_to_all, axis_name="views", split_axis=0, concat_axis=0, tiled=True
    )
    arrived = [swap(packed[0])]
    meta = swap(packed[parts].reshape(owners, CAP)).reshape(slots)
    arrived += [swap(packed[p]) for p in range(1, parts)]

    turned = jnp.swapaxes(reference_rows, 1, 2)
    padded = jnp.pad(turned, ((0, 0), (1, 1), (0, 0)))
    taps = jnp.repeat(conv_weight.transpose(1, 2, 3, 0).reshape(9, 3, -1), CG, axis=2) / CG
    edges = jnp.pad(conv_weight[..., 2], ((0, 0), (0, 0), (0, 5))).reshape(-1, 24) / CG
    edges = jnp.repeat(jnp.roll(jnp.pad(edges, ((0, 0), (0, pixels - 24))), -2, 1), CG, axis=0)
    total = None
    for p in range(parts):
        part = slice(p * width, (p + 1) * width)
        left = jnp.concatenate([padded[:, e : e + pixels, part] for e in range(3)], axis=2)
        weight = taps[:, :, part].reshape(9, 3 * width)
        total = add_chunk(p == 0, p == parts - 1, meta, arrived[p], left, weight, edges[part], total)

    ends = owners - 1
    before = lax.ppermute(total[rows + 1 :], "views", [(i, i + 1) for i in range(ends)])
    after = lax.ppermute(total[:1], "views", [(i + 1, i) for i in range(ends)])
    return depth_rows(total, before, after)


def solution(mesh):
    in_specs = (
        P(("groups", "views"), None, None),
        P(("groups", "views"), None),
        P(("groups", "views")),
        P(("groups", "views")),
        P(("groups", "views"), None, None),
        P(),
    )
    out_specs = P(("groups", "views"), None)
    return jax.shard_map(body, mesh=mesh, in_specs=in_specs, out_specs=out_specs, check_vma=False)
```

```python
import functools

import jax
import jax.numpy as jnp
from jax import lax
from jax.experimental import pallas as pl
from jax.experimental.pallas import tpu as pltpu
from jax.sharding import PartitionSpec as P

CG = 8
DISP = 96
DSPAN = 16
CAP = 2
SETS = 2

VMEM = pl.BlockSpec(memory_space=pltpu.VMEM)
SMEM = pl.BlockSpec(memory_space=pltpu.SMEM)
ANY = pl.BlockSpec(memory_space=pl.ANY)


def pack_kernel(half, span, code_ref, source_ref, out_ref, count_ref, sem):
    items = source_ref.shape[0]

    @pl.loop(0, half * SETS)
    def _(s):
        count_ref[s] = 0

    @pl.loop(0, items)
    def _(i):
        owner = lax.div(code_ref[i], span)
        place = lax.rem(owner, half) * SETS + lax.div(owner, half)
        slot = place * CAP + count_ref[place]
        count_ref[place] = count_ref[place] + 1
        pltpu.make_async_copy(source_ref.at[i], out_ref.at[slot], sem).start()

    @pl.loop(0, items)
    def _(i):
        pltpu.make_async_copy(source_ref.at[0], out_ref.at[0], sem).wait()


def pack_rows(codes, source, half, span):
    items, channels, pixels = source.shape
    slots = half * SETS * CAP
    return pl.pallas_call(
        functools.partial(pack_kernel, half, span),
        out_shape=jax.ShapeDtypeStruct((slots, channels, pixels), source.dtype),
        in_specs=[SMEM, VMEM],
        out_specs=ANY,
        scratch_shapes=[pltpu.SMEM((half * SETS,), jnp.int32), pltpu.SemaphoreType.DMA],
        name="pack_rows",
    )(codes, source)


def table_kernel(half, rows, code_ref, table_ref, state_ref):
    views, items = code_ref.shape
    span = rows * DSPAN
    room = half * CAP
    me = lax.axis_index("views")
    owners = (me, lax.rem(me + half, views))

    @pl.loop(0, SETS + SETS * rows)
    def _(j):
        table_ref[SETS * room + j] = 0

    @pl.loop(0, views)
    def _(p):
        home = lax.rem(me ^ p, half)
        for t in range(SETS):
            state_ref[t] = 0

        @pl.loop(0, items)
        def _(i):
            owner = lax.div(code_ref[p, i], span)
            rest = lax.rem(code_ref[p, i], span)
            for t in range(SETS):

                @pl.when(owner == owners[t])
                def _():
                    count = SETS * room + SETS + t * rows + lax.div(rest, DSPAN)
                    table_ref[count] = table_ref[count] + 1

                    @pl.when(p < half)
                    def _():
                        place = home * SETS + lax.div(owners[t], half)
                        entry = table_ref[SETS * room + t]
                        slot = place * CAP + state_ref[t]
                        table_ref[t * room + entry] = slot * span + rest
                        table_ref[SETS * room + t] = entry + 1
                        state_ref[t] = state_ref[t] + 1


def make_table(codes, half, rows):
    length = SETS * (half * CAP + 1 + rows)
    return pl.pallas_call(
        functools.partial(table_kernel, half, rows),
        out_shape=jax.ShapeDtypeStruct((length,), jnp.int32),
        in_specs=[SMEM],
        out_specs=SMEM,
        scratch_shapes=[pltpu.SMEM((SETS,), jnp.int32)],
        name="make_table",
    )(codes)


def split_two(values):
    high = values.astype(jnp.bfloat16)
    return high, (values - high.astype(jnp.float32)).astype(jnp.bfloat16)


def both_parts(values):
    return jnp.concatenate(split_two(values), axis=1)


def shift_left(values, offset):
    lane = lax.broadcasted_iota(jnp.int32, values.shape, 1)
    pixels = values.shape[1]
    moved = pltpu.roll(values, (-offset) % pixels, 1)
    return jnp.where((lane + offset >= 0) & (lane + offset < pixels), moved, 0.0)


def spread(values):
    groups, pixels = values.shape
    wide = jnp.broadcast_to(values[:, None, :], (groups, CG, pixels))
    return wide.reshape(groups * CG, pixels)


def set_kernel(
    t, room, table_ref, arrived_ref, left_ref, weight_ref, edge_ref,
    main_ref, low_ref, high_ref, stack_ref, wide_ref, total_ref, canvas_ref,
):
    slots, channels, pixels = arrived_ref.shape
    rows = left_ref.shape[0]
    span = rows * DSPAN
    lane = lax.broadcasted_iota(jnp.int32, (channels, pixels), 1)
    total_ref[...] = jnp.zeros_like(total_ref)
    canvas_ref[...] = jnp.zeros_like(canvas_ref)

    def add_slot(entry, carry):
        code = table_ref[t * room + entry]
        slot = lax.div(code, span)
        row = lax.div(lax.rem(code, span), DSPAN)
        begin = lax.rem(code, DSPAN)
        moved = pltpu.roll(arrived_ref[slot].astype(jnp.float32), begin, 1)
        canvas_ref[row] = canvas_ref[row] + jnp.where(lane >= begin, moved, 0.0)
        return carry

    lax.fori_loop(0, table_ref[SETS * room + t], add_slot, 0)

    @pl.loop(0, rows)
    def _(r):
        count = table_ref[SETS * room + SETS + t * rows + r]
        divisor = jnp.full((channels, pixels), jnp.maximum(count, 1).astype(jnp.float32))
        mean = canvas_ref[r] / divisor
        for e in range(3):
            stack_ref[r, e * channels : (e + 1) * channels, :] = shift_left(mean, e - 1)
        edge = jnp.broadcast_to(mean[:, :1], (channels, pixels)) * spread(edge_ref[...])
        wide = jnp.dot(
            left_ref[r, :, 2 * channels :],
            both_parts(edge),
            preferred_element_type=jnp.float32,
        )
        total_ref[(rows + 2) * 3 + r] = wide[:, :pixels] + wide[:, pixels:]

    @pl.loop(0, 9)
    def _(tap):
        wide_ref[...] = spread(weight_ref[tap])
        for r in range(rows):
            right = both_parts(stack_ref[r] * wide_ref[...])
            wide = jnp.dot(left_ref[r], right, preferred_element_type=jnp.float32)
            place = (r + 2 - lax.div(tap, 3)) * 3 + lax.rem(tap, 3)
            total_ref[place] = total_ref[place] + (wide[:, :pixels] + wide[:, pixels:])

    x = lax.broadcasted_iota(jnp.int32, (pixels, pixels), 0)
    v = lax.broadcasted_iota(jnp.int32, (pixels, pixels), 1)
    inside = (x >= v) & (x - v < DISP)
    border = (x < DISP - 1) & ((v >= pixels - 2) | (v < 1))
    for r in range(rows + 2):
        total = jnp.where(inside, total_ref[3 * r + 1], 0.0)
        for b in (0, 2):
            kept = jnp.where(inside, total_ref[3 * r + b], 0.0)
            total = total + pltpu.roll(kept, (b - 1) % pixels, 1)
        for a in range(3):
            if 0 <= r + a - 2 < rows:
                edge = total_ref[(rows + 2) * 3 + r + a - 2]
                moved = pltpu.roll(edge, (-8 * a) % pixels, 1) if a else edge
                total = total + jnp.where(border, moved, 0.0)
        step = 1
        while step < pixels:
            moved = pltpu.roll(total, pixels - step, 1)
            total = jnp.where(((x + 1) & step) != 0, moved, total)
            step *= 2
        kept = total.T[pixels - DISP :]
        if r == 0:
            low_ref[0] = kept
        elif r == rows + 1:
            high_ref[0] = kept
        else:
            main_ref[r - 1] = kept


def add_set(t, table, arrived, left, weight, edge):
    slots, channels, pixels = arrived.shape
    rows = left.shape[0]
    room = slots // SETS
    shapes = [(n, DISP, pixels) for n in (rows, 1, 1)]
    return pl.pallas_call(
        functools.partial(set_kernel, t, room),
        out_shape=[jax.ShapeDtypeStruct(shape, jnp.float32) for shape in shapes],
        in_specs=[SMEM] + [VMEM] * 4,
        out_specs=[VMEM] * 3,
        scratch_shapes=[
            pltpu.VMEM((rows, 3 * channels, pixels), jnp.float32),
            pltpu.VMEM((3 * channels, pixels), jnp.float32),
            pltpu.VMEM(((rows + 2) * 3 + rows, pixels, pixels), jnp.float32),
            pltpu.VMEM((rows, channels, pixels), jnp.float32),
        ],
        cost_estimate=pl.CostEstimate(
            flops=2 * rows * 9 * pixels * 2 * pixels * 3 * channels,
            bytes_accessed=2 * slots * channels * pixels,
            transcendentals=0,
        ),
        name="add_set",
    )(table, arrived, left, weight, edge)


def depth_kernel(own_ref, far_ref, before_ref, before_far_ref, after_ref, after_far_ref, out_ref):
    rows, pixels = out_ref.shape
    level = (DISP - 1) - lax.broadcasted_iota(jnp.int32, (DISP, pixels), 0)
    share = level.astype(jnp.float32) / DISP
    for r in range(rows):
        scores = own_ref[r] + far_ref[r]
        if r == 0:
            scores = scores + (before_ref[0] + before_far_ref[0])
        if r == rows - 1:
            scores = scores + (after_ref[0] + after_far_ref[0])
        weights = jnp.exp(scores - jnp.max(scores, axis=0, keepdims=True))
        bottom = jnp.sum(weights, axis=0, keepdims=True)
        out_ref[r : r + 1, :] = jnp.sum(weights * share, axis=0, keepdims=True) / bottom


def depth_rows(*parts):
    rows, _, pixels = parts[0].shape
    return pl.pallas_call(
        depth_kernel,
        out_shape=jax.ShapeDtypeStruct((rows, pixels), jnp.float32),
        in_specs=[VMEM] * len(parts),
        out_specs=VMEM,
        name="depth_rows",
    )(*parts)


def stack_left(reference_rows):
    pixels = reference_rows.shape[2]
    padded = jnp.pad(jnp.swapaxes(reference_rows, 1, 2), ((0, 0), (1, 1), (0, 0)))
    return jnp.concatenate([padded[:, e : e + pixels] for e in range(3)], axis=2)


def gather_codes(codes, views):
    gathered = codes[None]
    step = 1
    while step < views:
        other = lax.ppermute(gathered, "views", [(i, i ^ step) for i in range(views)])
        gathered = jnp.concatenate([gathered, other], axis=0)
        step *= 2
    return gathered


def body(source_rows, route_owner, target_row, start_index, reference_rows, conv_weight):
    views = lax.axis_size("views")
    half = views // 2
    rows, channels, pixels = reference_rows.shape
    span = rows * DSPAN
    send = functools.partial(lax.ppermute, axis_name="views")
    far_rows = send(reference_rows, perm=[(i, (i + half) % views) for i in range(views)])
    codes = route_owner[:, 0] * span + target_row * DSPAN + start_index
    packed = pack_rows(codes, source_rows, half, span)
    arrived = lax.all_to_all(
        packed,
        "views",
        split_axis=0,
        concat_axis=0,
        tiled=True,
        axis_index_groups=[list(range(half)), list(range(half, views))],
    )
    table = make_table(gather_codes(codes, views), half, rows)

    scaled = conv_weight / CG
    taps = scaled.transpose(1, 2, 3, 0).reshape(9, -1, 1)
    taps = jnp.broadcast_to(taps, taps.shape[:2] + (pixels,))
    edges = jnp.pad(scaled[..., 2], ((0, 0), (0, 0), (0, 5))).reshape(-1, 24)
    edges = jnp.roll(jnp.pad(edges, ((0, 0), (0, pixels - 24))), -2, 1)
    near, far = stack_left(reference_rows), stack_left(far_rows)

    far_main, far_low, far_high = add_set(1, table, arrived, far, taps, edges)
    home = [(i, (i + half) % views) for i in range(views)]
    other_main = send(far_main, perm=home)
    other_low = send(far_low, perm=[(i, j - 1) for i, j in home if j > 0])
    other_high = send(far_high, perm=[(i, j + 1) for i, j in home if j + 1 < views])
    own_main, own_low, own_high = add_set(0, table, arrived, near, taps, edges)
    own_low = send(own_low, perm=[(i, i - 1) for i in range(1, views)])
    own_high = send(own_high, perm=[(i, i + 1) for i in range(views - 1)])
    return depth_rows(own_main, other_main, own_high, other_high, own_low, other_low)


def solution(mesh):
    in_specs = (
        P(("groups", "views"), None, None),
        P(("groups", "views"), None),
        P(("groups", "views")),
        P(("groups", "views")),
        P(("groups", "views"), None, None),
        P(),
    )
    out_specs = P(("groups", "views"), None)
    return jax.shard_map(body, mesh=mesh, in_specs=in_specs, out_specs=out_specs, check_vma=False)
```

```python
import functools

import jax
import jax.numpy as jnp
from jax import lax
from jax.experimental import pallas as pl
from jax.experimental.pallas import tpu as pltpu
from jax.sharding import PartitionSpec as P


CG = 8
DISP = 96
DSPAN = 16
CAP = 2
SETS = 2

VMEM = pl.BlockSpec(memory_space=pltpu.VMEM)
SMEM = pl.BlockSpec(memory_space=pltpu.SMEM)
ANY = pl.BlockSpec(memory_space=pl.ANY)


def pack_kernel(half, span, code_ref, source_ref, out_ref, count_ref, sem):
    items = source_ref.shape[0]

    @pl.loop(0, half * SETS)
    def _(s):
        count_ref[s] = 0

    @pl.loop(0, items)
    def _(i):
        owner = lax.div(code_ref[i], span)
        place = lax.rem(owner, half) * SETS + lax.div(owner, half)
        slot = place * CAP + count_ref[place]
        count_ref[place] = count_ref[place] + 1
        pltpu.make_async_copy(source_ref.at[i], out_ref.at[slot], sem).start()

    @pl.loop(0, items)
    def _(i):
        pltpu.make_async_copy(source_ref.at[0], out_ref.at[0], sem).wait()


def pack_rows(codes, source, half, span):
    _, channels, pixels = source.shape
    slots = half * SETS * CAP
    return pl.pallas_call(
        functools.partial(pack_kernel, half, span),
        out_shape=jax.ShapeDtypeStruct((slots, channels, pixels), source.dtype),
        in_specs=[SMEM, VMEM],
        out_specs=ANY,
        scratch_shapes=[pltpu.SMEM((half * SETS,), jnp.int32), pltpu.SemaphoreType.DMA],
        name="pack_rows",
    )(codes, source)


def table_kernel(half, rows, code_ref, table_ref, state_ref):
    views, items = code_ref.shape
    span = rows * DSPAN
    room = half * CAP
    me = lax.axis_index("views")
    owners = (me, lax.rem(me + half, views))

    @pl.loop(0, SETS + SETS * rows)
    def _(j):
        table_ref[SETS * room + j] = 0

    @pl.loop(0, views)
    def _(p):
        home = lax.rem(me ^ p, half)
        for t in range(SETS):
            state_ref[t] = 0

        @pl.loop(0, items)
        def _(i):
            owner = lax.div(code_ref[p, i], span)
            rest = lax.rem(code_ref[p, i], span)
            for t in range(SETS):

                @pl.when(owner == owners[t])
                def _():
                    count = SETS * room + SETS + t * rows + lax.div(rest, DSPAN)
                    table_ref[count] = table_ref[count] + 1

                    @pl.when(p < half)
                    def _():
                        place = home * SETS + lax.div(owners[t], half)
                        entry = table_ref[SETS * room + t]
                        slot = place * CAP + state_ref[t]
                        table_ref[t * room + entry] = slot * span + rest
                        table_ref[SETS * room + t] = entry + 1
                        state_ref[t] = state_ref[t] + 1


def make_table(codes, half, rows):
    length = SETS * (half * CAP + 1 + rows)
    return pl.pallas_call(
        functools.partial(table_kernel, half, rows),
        out_shape=jax.ShapeDtypeStruct((length,), jnp.int32),
        in_specs=[SMEM],
        out_specs=SMEM,
        scratch_shapes=[pltpu.SMEM((SETS,), jnp.int32)],
        name="make_table",
    )(codes)


def split_two(values):
    high = values.astype(jnp.bfloat16)
    return high, (values - high.astype(jnp.float32)).astype(jnp.bfloat16)


def both_parts(values):
    return jnp.concatenate(split_two(values), axis=1)


def shift_left(values, offset):
    lane = lax.broadcasted_iota(jnp.int32, values.shape, 1)
    pixels = values.shape[1]
    moved = pltpu.roll(values, (-offset) % pixels, 1)
    return jnp.where((lane + offset >= 0) & (lane + offset < pixels), moved, 0.0)


def set_kernel(
    t, table_ref, arrived_ref, left_ref, weight_ref, edge_ref, main_ref, low_ref, high_ref,
    slot_ref, stack_ref, total_ref, canvas_ref, sems,
):
    room, channels, pixels = slot_ref.shape
    rows = left_ref.shape[0]
    span = rows * DSPAN
    tap = pl.program_id(0)
    entries = table_ref[SETS * room + t]

    def slot_copy(entry):
        slot = lax.div(table_ref[t * room + entry], span)
        return pltpu.make_async_copy(arrived_ref.at[slot], slot_ref.at[entry], sems.at[entry])

    @pl.when(tap == 0)
    def _():
        lane = lax.broadcasted_iota(jnp.int32, (channels, pixels), 1)

        @pl.loop(0, entries)
        def _(entry):
            slot_copy(entry).start()

        total_ref[...] = jnp.zeros_like(total_ref)
        canvas_ref[...] = jnp.zeros_like(canvas_ref)

        @pl.loop(0, entries)
        def _(entry):
            slot_copy(entry).wait()
            rest = lax.rem(table_ref[t * room + entry], span)
            row = lax.div(rest, DSPAN)
            begin = lax.rem(rest, DSPAN)
            moved = pltpu.roll(slot_ref[entry].astype(jnp.float32), begin, 1)
            canvas_ref[row] = canvas_ref[row] + jnp.where(lane >= begin, moved, 0.0)

        @pl.loop(0, rows)
        def _(r):
            count = table_ref[SETS * room + SETS + t * rows + r]
            divisor = jnp.full((channels, pixels), jnp.maximum(count, 1).astype(jnp.float32))
            mean = canvas_ref[r] / divisor
            for e in range(3):
                stack_ref[r, e * channels : (e + 1) * channels, :] = shift_left(mean, e - 1)
            edge = jnp.broadcast_to(mean[:, :1], (channels, pixels)) * edge_ref[...]
            wide = jnp.dot(
                left_ref[r, :, 2 * channels :],
                both_parts(edge),
                preferred_element_type=jnp.float32,
            )
            total_ref[(rows + 2) * 3 + r] = wide[:, :pixels] + wide[:, pixels:]

    for r in range(rows):
        right = both_parts(stack_ref[r] * weight_ref[0])
        wide = jnp.dot(left_ref[r], right, preferred_element_type=jnp.float32)
        place = (r + 2 - lax.div(tap, 3)) * 3 + lax.rem(tap, 3)
        total_ref[place] = total_ref[place] + (wide[:, :pixels] + wide[:, pixels:])

    @pl.when(tap == pl.num_programs(0) - 1)
    def _():
        x = pixels - 1 - lax.broadcasted_iota(jnp.int32, (pixels, pixels), 0)
        v = lax.broadcasted_iota(jnp.int32, (pixels, pixels), 1)
        inside = (x >= v) & (x - v < DISP)
        border = (x < DISP - 1) & ((v >= pixels - 2) | (v < 1))
        for r in range(rows + 2):
            total = jnp.where(inside, total_ref[3 * r + 1], 0.0)
            for b in (0, 2):
                kept = jnp.where(inside, total_ref[3 * r + b], 0.0)
                total = total + pltpu.roll(kept, (b - 1) % pixels, 1)
            for a in range(3):
                if 0 <= r + a - 2 < rows:
                    edge = total_ref[(rows + 2) * 3 + r + a - 2]
                    moved = pltpu.roll(edge, (-8 * a) % pixels, 1) if a else edge
                    total = total + jnp.where(border, moved, 0.0)
            total = pltpu.roll(total, 0, 1, stride=1, stride_axis=0)
            kept = total.T[pixels - DISP :]
            if r == 0:
                low_ref[0] = kept
            elif r == rows + 1:
                high_ref[0] = kept
            else:
                main_ref[r - 1] = kept


def add_set(t, table, arrived, left, weight, edge):
    slots, channels, pixels = arrived.shape
    rows = left.shape[0]
    room = slots // SETS
    shapes = [(n, DISP, pixels) for n in (rows, 1, 1)]
    once = pl.Buffered(1)
    return pl.pallas_call(
        functools.partial(set_kernel, t),
        grid=(weight.shape[0],),
        out_shape=[jax.ShapeDtypeStruct(shape, jnp.float32) for shape in shapes],
        in_specs=[
            SMEM,
            ANY,
            pl.BlockSpec(left.shape, lambda tap: (0, 0, 0), pipeline_mode=once),
            pl.BlockSpec((1,) + weight.shape[1:], lambda tap: (tap, 0, 0)),
            pl.BlockSpec(edge.shape, lambda tap: (0, 0), pipeline_mode=once),
        ],
        out_specs=[pl.BlockSpec(shape, lambda tap: (0, 0, 0)) for shape in shapes],
        scratch_shapes=[
            pltpu.VMEM((room, channels, pixels), arrived.dtype),
            pltpu.VMEM((rows, 3 * channels, pixels), jnp.float32),
            pltpu.VMEM(((rows + 2) * 3 + rows, pixels, pixels), jnp.float32),
            pltpu.VMEM((rows, channels, pixels), jnp.float32),
            pltpu.SemaphoreType.DMA((room,)),
        ],
        compiler_params=pltpu.CompilerParams(vmem_limit_bytes=24 << 20),
        cost_estimate=pl.CostEstimate(
            flops=2 * rows * 9 * pixels * 2 * pixels * 3 * channels,
            bytes_accessed=2 * slots * channels * pixels,
            transcendentals=0,
        ),
        name="add_set",
    )(table, arrived, left, weight, edge)


def depth_kernel(own_ref, far_ref, before_ref, before_far_ref, after_ref, after_far_ref, out_ref):
    rows, pixels = out_ref.shape
    level = (DISP - 1) - lax.broadcasted_iota(jnp.int32, (DISP, pixels), 0)
    share = level.astype(jnp.float32) / DISP
    depths = []
    for r in range(rows):
        scores = own_ref[r] + far_ref[r]
        if r == 0:
            scores = scores + (before_ref[0] + before_far_ref[0])
        if r == rows - 1:
            scores = scores + (after_ref[0] + after_far_ref[0])
        weights = jnp.exp(scores - jnp.max(scores, axis=0, keepdims=True))
        bottom = jnp.sum(weights, axis=0, keepdims=True)
        depths.append(jnp.sum(weights * share, axis=0, keepdims=True) / bottom)
    lane = lax.broadcasted_iota(jnp.int32, (8, pixels), 1)
    depth = jnp.concatenate(depths + [depths[0]] * (-rows % 8), axis=0)
    out_ref[...] = jnp.take_along_axis(depth, pixels - 1 - lane, axis=1)[:rows]


def depth_rows(*parts):
    rows, _, pixels = parts[0].shape
    return pl.pallas_call(
        depth_kernel,
        out_shape=jax.ShapeDtypeStruct((rows, pixels), jnp.float32),
        in_specs=[VMEM] * len(parts),
        out_specs=VMEM,
        name="depth_rows",
    )(*parts)


def stack_left(reference_rows):
    pixels = reference_rows.shape[2]
    padded = jnp.pad(jnp.swapaxes(reference_rows, 1, 2), ((0, 0), (1, 1), (0, 0)))
    return jnp.concatenate([padded[:, e : e + pixels] for e in range(3)], axis=2)[:, ::-1]


def gather_codes(codes, views):
    bits = views.bit_length() - 1
    gathered = codes[None]
    digits = 0
    while bits:
        width = min(2, bits)
        bits -= width
        moved = [
            lax.ppermute(gathered, "views", [(i, i ^ (k << bits)) for i in range(views)])
            for k in range(1, 1 << width)
        ]
        gathered = jnp.stack([gathered] + moved)
        digits += 1
    order = tuple(range(digits))[::-1] + (digits, digits + 1)
    return gathered.transpose(order).reshape(views, -1)


def compute(source_rows, route_owner, target_row, start_index, reference_rows, conv_weight):
    views = lax.axis_size("views")
    half = views // 2
    rows, _, pixels = reference_rows.shape
    span = rows * DSPAN
    send = functools.partial(lax.ppermute, axis_name="views")
    home = [(i, (i + half) % views) for i in range(views)]
    codes = route_owner[:, 0] * span + target_row * DSPAN + start_index
    far_rows = send(reference_rows, perm=home)
    packed = pack_rows(codes, source_rows, half, span)
    arrived = lax.all_to_all(
        packed,
        "views",
        split_axis=0,
        concat_axis=0,
        tiled=True,
        axis_index_groups=[list(range(half)), list(range(half, views))],
    )
    table = make_table(gather_codes(codes, views), half, rows)

    scaled = jnp.repeat(conv_weight / CG, CG, axis=0)
    taps = scaled.transpose(1, 2, 3, 0).reshape(9, -1, 1)
    taps = jnp.broadcast_to(taps, taps.shape[:2] + (pixels,))
    edges = jnp.pad(scaled[..., 2], ((0, 0), (0, 0), (0, 5))).reshape(-1, 24)
    edges = jnp.roll(jnp.pad(edges, ((0, 0), (0, pixels - 24))), -2, 1)
    near, far = stack_left(reference_rows), stack_left(far_rows)

    far_main, far_low, far_high = add_set(1, table, arrived, far, taps, edges)
    other_main = send(far_main, perm=home)
    other_low = send(far_low, perm=[(i, j - 1) for i, j in home if j > 0])
    other_high = send(far_high, perm=[(i, j + 1) for i, j in home if j + 1 < views])
    own_main, own_low, own_high = add_set(0, table, arrived, near, taps, edges)
    own_low = send(own_low, perm=[(i, i - 1) for i in range(1, views)])
    own_high = send(own_high, perm=[(i, i + 1) for i in range(views - 1)])
    return depth_rows(own_main, other_main, own_high, other_high, own_low, other_low)


def solution(mesh):
    in_specs = (
        P(("groups", "views"), None, None),
        P(("groups", "views"), None),
        P(("groups", "views")),
        P(("groups", "views")),
        P(("groups", "views"), None, None),
        P(),
    )
    out_specs = P(("groups", "views"), None)
    return jax.shard_map(compute, mesh=mesh, in_specs=in_specs, out_specs=out_specs, check_vma=False)
```

```python
import functools

import jax
import jax.numpy as jnp
from jax import lax
from jax.experimental import pallas as pl
from jax.experimental.pallas import tpu as pltpu
from jax.sharding import PartitionSpec as P


CG = 8
DISP = 96
DSPAN = 16
CAP = 2
SETS = 2

VMEM = pl.BlockSpec(memory_space=pltpu.VMEM)
SMEM = pl.BlockSpec(memory_space=pltpu.SMEM)
ANY = pl.BlockSpec(memory_space=pl.ANY)


def pack_kernel(
    half, span, code_ref, source_ref, note_ref, far_ref, own_ref,
    count_ref, slot_ref, block_ref, sem,
):
    items, channels, pixels = source_ref.shape
    outs = (own_ref, far_ref)
    side = lax.div(lax.axis_index("views"), half)
    lane = lax.broadcasted_iota(jnp.int32, (1, pixels), 1)
    slot_ref[...] = jnp.full_like(slot_ref, -1.0)

    @pl.loop(0, SETS * half)
    def _(j):
        count_ref[j] = 0

    @pl.loop(0, items)
    def _(i):
        owner = lax.div(code_ref[i], span)
        rest = lax.rem(code_ref[i], span)
        home = lax.rem(owner, half)
        for t in range(SETS):

            @pl.when((lax.div(owner, half) == side) == (t == 0))
            def _():
                place = count_ref[t * half + home]
                count_ref[t * half + home] = place + 1
                first = pl.multiple_of(place * channels, channels)
                pltpu.make_async_copy(
                    source_ref.at[i], outs[t].at[home, pl.ds(first, channels), :], sem
                ).start()
                value = jnp.full((1, pixels), rest.astype(jnp.float32))
                line = slot_ref[pl.ds(home, 1), :]
                slot_ref[pl.ds(home, 1), :] = jnp.where(lane == t * CAP + place, value, line)

    height = note_ref.shape[0]
    row = lax.broadcasted_iota(jnp.int32, (height, pixels), 0)
    note = note_ref[...].astype(jnp.float32)

    @pl.loop(0, half)
    def _(j):
        line = jnp.broadcast_to(slot_ref[pl.ds(j, 1), :], (height, pixels))
        block_ref[j] = jnp.where(row == 4, line, note).astype(block_ref.dtype)

    last = pltpu.make_async_copy(
        block_ref, far_ref.at[:, pl.ds(CAP * channels, height), :], sem
    )
    last.start()

    @pl.loop(0, items)
    def _(i):
        pltpu.make_async_copy(
            source_ref.at[0], own_ref.at[0, pl.ds(0, channels), :], sem
        ).wait()

    last.wait()


def pack_rows(codes, source, note, half, span):
    _, channels, pixels = source.shape
    height = note.shape[0]
    lengths = (CAP * channels + height, CAP * channels)
    return pl.pallas_call(
        functools.partial(pack_kernel, half, span),
        out_shape=[jax.ShapeDtypeStruct((half, n, pixels), source.dtype) for n in lengths],
        in_specs=[SMEM, VMEM, VMEM],
        out_specs=[ANY, ANY],
        scratch_shapes=[
            pltpu.SMEM((SETS * half,), jnp.int32),
            pltpu.VMEM((half, pixels), jnp.float32),
            pltpu.VMEM((half, height, pixels), source.dtype),
            pltpu.SemaphoreType.DMA,
        ],
        compiler_params=pltpu.CompilerParams(vmem_limit_bytes=24 << 20),
        name="pack_rows",
    )(codes, source, note)


def left_kernel(reference_ref, left_ref):
    rows, channels, pixels = reference_ref.shape
    i = lax.broadcasted_iota(jnp.int32, (pixels, pixels), 0)
    x = lax.broadcasted_iota(jnp.int32, (pixels, pixels), 1)
    for e in range(3):
        pick = jnp.where(x == pixels - 1 - i + (e - 1), 1.0, 0.0).astype(jnp.bfloat16)
        for r in range(rows):
            moved = lax.dot_general(
                pick,
                reference_ref[r],
                (((1,), (1,)), ((), ())),
                preferred_element_type=jnp.float32,
            )
            left_ref[r, :, e * channels : (e + 1) * channels] = moved.astype(left_ref.dtype)


def stack_left(reference):
    rows, channels, pixels = reference.shape
    return pl.pallas_call(
        left_kernel,
        out_shape=jax.ShapeDtypeStruct((rows, pixels, 3 * channels), reference.dtype),
        in_specs=[VMEM],
        out_specs=VMEM,
        compiler_params=pltpu.CompilerParams(vmem_limit_bytes=24 << 20),
        name="stack_left",
    )(reference)


def split_two(values):
    high = values.astype(jnp.bfloat16)
    return high, (values - high.astype(jnp.float32)).astype(jnp.bfloat16)


def both_parts(values):
    return jnp.concatenate(split_two(values), axis=1)


def shift_left(values, offset):
    lane = lax.broadcasted_iota(jnp.int32, values.shape, 1)
    pixels = values.shape[1]
    moved = pltpu.roll(values, (-offset) % pixels, 1)
    return jnp.where((lane + offset >= 0) & (lane + offset < pixels), moved, 0.0)


def set_kernel(
    t, code_ref, arrived_ref, note_ref, left_ref, weight_ref, edge_ref,
    main_ref, low_ref, high_ref, slot_ref, stack_ref, total_ref, canvas_ref, sems,
):
    room, channels, pixels = slot_ref.shape
    rows = left_ref.shape[0]
    half = note_ref.shape[0]
    tap = pl.program_id(0)

    def slot_code(entry):
        return code_ref[lax.div(entry, CAP) * (SETS * CAP) + t * CAP + lax.rem(entry, CAP)]

    def slot_copy(entry):
        first = pl.multiple_of(lax.rem(entry, CAP) * channels, channels)
        return pltpu.make_async_copy(
            arrived_ref.at[lax.div(entry, CAP), pl.ds(first, channels), :],
            slot_ref.at[entry],
            sems.at[entry],
        )

    @pl.when(tap == 0)
    def _():
        lane = lax.broadcasted_iota(jnp.int32, (channels, pixels), 1)

        @pl.loop(0, room)
        def _(entry):
            @pl.when(slot_code(entry) >= 0)
            def _():
                slot_copy(entry).start()

        total_ref[...] = jnp.zeros_like(total_ref)
        canvas_ref[...] = jnp.zeros_like(canvas_ref)
        owner = lax.rem(lax.axis_index("views") + t * half, SETS * half)
        counts = [0.0] * rows
        for first in (0, 2):
            named = note_ref[:, first, :].astype(jnp.float32).astype(jnp.int32) == owner
            row = lax.div(note_ref[:, first + 1, :].astype(jnp.float32).astype(jnp.int32), DSPAN)
            for r in range(rows):
                counts[r] = counts[r] + jnp.where(named & (row == r), 1.0, 0.0)
        counts = [jnp.maximum(jnp.sum(count), 1.0) for count in counts]

        @pl.loop(0, room)
        def _(entry):
            code = slot_code(entry)

            @pl.when(code >= 0)
            def _():
                slot_copy(entry).wait()
                row = lax.div(code, DSPAN)
                begin = lax.rem(code, DSPAN)
                moved = pltpu.roll(slot_ref[entry].astype(jnp.float32), begin, 1)
                canvas_ref[row] = canvas_ref[row] + jnp.where(lane >= begin, moved, 0.0)

        for r in range(rows):
            mean = canvas_ref[r] / jnp.full((channels, pixels), counts[r])
            for e in range(3):
                stack_ref[r, e * channels : (e + 1) * channels, :] = shift_left(mean, e - 1)
            edge = jnp.broadcast_to(mean[:, :1], (channels, pixels)) * edge_ref[...]
            wide = jnp.dot(
                left_ref[r, :, 2 * channels :],
                both_parts(edge),
                preferred_element_type=jnp.float32,
            )
            total_ref[(rows + 2) * 3 + r] = wide[:, :pixels] + wide[:, pixels:]

    for r in range(rows):
        right = both_parts(stack_ref[r] * weight_ref[0])
        wide = jnp.dot(left_ref[r], right, preferred_element_type=jnp.float32)
        place = (r + 2 - lax.div(tap, 3)) * 3 + lax.rem(tap, 3)
        total_ref[place] = total_ref[place] + (wide[:, :pixels] + wide[:, pixels:])

    @pl.when(tap == pl.num_programs(0) - 1)
    def _():
        x = pixels - 1 - lax.broadcasted_iota(jnp.int32, (pixels, pixels), 0)
        v = lax.broadcasted_iota(jnp.int32, (pixels, pixels), 1)
        inside = (x >= v) & (x - v < DISP)
        border = (x < DISP - 1) & ((v >= pixels - 2) | (v < 1))
        for r in range(rows + 2):
            total = jnp.where(inside, total_ref[3 * r + 1], 0.0)
            for b in (0, 2):
                kept = jnp.where(inside, total_ref[3 * r + b], 0.0)
                total = total + pltpu.roll(kept, (b - 1) % pixels, 1)
            for a in range(3):
                if 0 <= r + a - 2 < rows:
                    edge = total_ref[(rows + 2) * 3 + r + a - 2]
                    moved = pltpu.roll(edge, (-8 * a) % pixels, 1) if a else edge
                    total = total + jnp.where(border, moved, 0.0)
            total = pltpu.roll(total, 0, 1, stride=1, stride_axis=0)
            kept = total.T[pixels - DISP :]
            if r == 0:
                low_ref[0] = kept
            elif r == rows + 1:
                high_ref[0] = kept
            else:
                main_ref[r - 1] = kept


def add_set(t, codes, arrived, note, left, weight, edge):
    rows, pixels, depth = left.shape
    channels = depth // 3
    half = arrived.shape[0]
    room = half * CAP
    shapes = [(n, DISP, pixels) for n in (rows, 1, 1)]
    once = pl.Buffered(1)
    return pl.pallas_call(
        functools.partial(set_kernel, t),
        grid=(weight.shape[0],),
        out_shape=[jax.ShapeDtypeStruct(shape, jnp.float32) for shape in shapes],
        in_specs=[
            SMEM,
            ANY,
            pl.BlockSpec(note.shape, lambda tap: (0, 0, 0), pipeline_mode=once),
            pl.BlockSpec(left.shape, lambda tap: (0, 0, 0), pipeline_mode=once),
            pl.BlockSpec((1,) + weight.shape[1:], lambda tap: (tap, 0, 0)),
            pl.BlockSpec(edge.shape, lambda tap: (0, 0), pipeline_mode=once),
        ],
        out_specs=[pl.BlockSpec(shape, lambda tap: (0, 0, 0)) for shape in shapes],
        scratch_shapes=[
            pltpu.VMEM((room, channels, pixels), arrived.dtype),
            pltpu.VMEM((rows, 3 * channels, pixels), jnp.float32),
            pltpu.VMEM(((rows + 2) * 3 + rows, pixels, pixels), jnp.float32),
            pltpu.VMEM((rows, channels, pixels), jnp.float32),
            pltpu.SemaphoreType.DMA((room,)),
        ],
        compiler_params=pltpu.CompilerParams(vmem_limit_bytes=24 << 20),
        cost_estimate=pl.CostEstimate(
            flops=2 * rows * 9 * pixels * 2 * pixels * 3 * channels,
            bytes_accessed=2 * room * channels * pixels,
            transcendentals=0,
        ),
        name="add_set",
    )(codes, arrived, note, left, weight, edge)


def depth_kernel(own_ref, far_ref, before_ref, before_far_ref, after_ref, after_far_ref, out_ref):
    rows, pixels = out_ref.shape
    level = (DISP - 1) - lax.broadcasted_iota(jnp.int32, (DISP, pixels), 0)
    share = level.astype(jnp.float32) / DISP
    depths = []
    for r in range(rows):
        scores = own_ref[r] + far_ref[r]
        if r == 0:
            scores = scores + (before_ref[0] + before_far_ref[0])
        if r == rows - 1:
            scores = scores + (after_ref[0] + after_far_ref[0])
        weights = jnp.exp(scores - jnp.max(scores, axis=0, keepdims=True))
        bottom = jnp.sum(weights, axis=0, keepdims=True)
        depths.append(jnp.sum(weights * share, axis=0, keepdims=True) / bottom)
    lane = lax.broadcasted_iota(jnp.int32, (8, pixels), 1)
    depth = jnp.concatenate(depths + [depths[0]] * (-rows % 8), axis=0)
    out_ref[...] = jnp.take_along_axis(depth, pixels - 1 - lane, axis=1)[:rows]


def depth_rows(*parts):
    rows, _, pixels = parts[0].shape
    return pl.pallas_call(
        depth_kernel,
        out_shape=jax.ShapeDtypeStruct((rows, pixels), jnp.float32),
        in_specs=[VMEM] * len(parts),
        out_specs=VMEM,
        compiler_params=pltpu.CompilerParams(vmem_limit_bytes=24 << 20),
        name="depth_rows",
    )(*parts)


def compute(source_rows, route_owner, target_row, start_index, reference_rows, conv_weight):
    views = lax.axis_size("views")
    half = views // 2
    rows, channels, pixels = reference_rows.shape
    span = rows * DSPAN
    send = functools.partial(lax.ppermute, axis_name="views")
    home = [(i, (i + half) % views) for i in range(views)]
    groups = [list(range(half)), list(range(half, views))]
    swap = functools.partial(
        lax.all_to_all,
        axis_name="views",
        split_axis=0,
        concat_axis=0,
        tiled=True,
        axis_index_groups=groups,
    )
    owner = route_owner[:, 0]
    rest = target_row * DSPAN + start_index
    named = jnp.stack([owner, rest]).astype(jnp.bfloat16)
    named = jnp.pad(named, ((0, 0), (0, pixels - named.shape[1])), constant_values=-1)
    far_named = send(named, perm=home)
    far_rows = send(reference_rows, perm=home)
    note = jnp.pad(jnp.concatenate([named, far_named]), ((0, 12), (0, 0)))
    packed_far, packed_own = pack_rows(owner * span + rest, source_rows, note, half, span)
    arrived_far = swap(packed_far)
    arrived_own = swap(packed_own)
    note = arrived_far[:, CAP * channels :]
    codes = note[:, 4, : SETS * CAP].astype(jnp.int32).reshape(-1)

    scaled = jnp.repeat(conv_weight / CG, CG, axis=0)
    taps = scaled.transpose(1, 2, 3, 0).reshape(9, -1, 1)
    taps = jnp.broadcast_to(taps, taps.shape[:2] + (pixels,))
    edges = jnp.pad(scaled[..., 2], ((0, 0), (0, 0), (0, 5))).reshape(-1, 24)
    edges = jnp.roll(jnp.pad(edges, ((0, 0), (0, pixels - 24))), -2, 1)
    near, far = stack_left(reference_rows), stack_left(far_rows)

    keep = functools.partial(pltpu.with_memory_space_constraint, memory_space=pltpu.HBM)
    taps, near, far = keep(taps), keep(near), keep(far)
    far_main, far_low, far_high = add_set(1, codes, arrived_far, note, far, taps, edges)
    other_main = send(far_main, perm=home)
    other_low = send(far_low, perm=[(i, j - 1) for i, j in home if j > 0])
    other_high = send(far_high, perm=[(i, j + 1) for i, j in home if j + 1 < views])
    own_main, own_low, own_high = add_set(0, codes, arrived_own, note, near, taps, edges)
    own_low = send(own_low, perm=[(i, i - 1) for i in range(1, views)])
    own_high = send(own_high, perm=[(i, i + 1) for i in range(views - 1)])
    return depth_rows(own_main, other_main, own_high, other_high, own_low, other_low)


def solution(mesh):
    in_specs = (
        P(("groups", "views"), None, None),
        P(("groups", "views"), None),
        P(("groups", "views")),
        P(("groups", "views")),
        P(("groups", "views"), None, None),
        P(),
    )
    out_specs = P(("groups", "views"), None)
    return jax.shard_map(compute, mesh=mesh, in_specs=in_specs, out_specs=out_specs, check_vma=False)
```

```python
import functools

import jax
import jax.numpy as jnp
from jax import lax
from jax.experimental import pallas as pl
from jax.experimental.pallas import tpu as pltpu
from jax.sharding import PartitionSpec as P


CG = 8
DISP = 96
DSPAN = 16
CAP = 2
SETS = 2

VMEM = pl.BlockSpec(memory_space=pltpu.VMEM)
SMEM = pl.BlockSpec(memory_space=pltpu.SMEM)
ANY = pl.BlockSpec(memory_space=pl.ANY)


def pack_kernel(
    half, span, code_ref, source_ref, note_ref, far_ref, *rest
):
    own_refs = rest[:-4]
    count_ref, slot_ref, block_ref, sem = rest[-4:]
    items, channels, pixels = source_ref.shape
    side = lax.div(lax.axis_index("views"), half)
    here = lax.rem(lax.axis_index("views"), half)
    lane = lax.broadcasted_iota(jnp.int32, (1, pixels), 1)
    slot_ref[...] = jnp.full_like(slot_ref, -1.0)

    @pl.loop(0, SETS * half)
    def _(j):
        count_ref[j] = 0

    @pl.loop(0, items)
    def _(i):
        owner = lax.div(code_ref[i], span)
        rest = lax.rem(code_ref[i], span)
        home = lax.rem(owner, half)
        for t in range(SETS):

            @pl.when((lax.div(owner, half) == side) == (t == 0))
            def _():
                place = count_ref[t * half + home]
                count_ref[t * half + home] = place + 1
                first = pl.multiple_of(place * channels, channels)
                if t == 0 and len(own_refs) > 1:
                    for k, own_ref in enumerate(own_refs):

                        @pl.when(home == here ^ k)
                        def _():
                            target = own_ref.at[pl.ds(first, channels), :]
                            pltpu.make_async_copy(source_ref.at[i], target, sem).start()
                else:
                    target = (own_refs[0], far_ref)[t].at[home, pl.ds(first, channels), :]
                    pltpu.make_async_copy(source_ref.at[i], target, sem).start()
                value = jnp.full((1, pixels), rest.astype(jnp.float32))
                line = slot_ref[pl.ds(home, 1), :]
                slot_ref[pl.ds(home, 1), :] = jnp.where(lane == t * CAP + place, value, line)

    height = note_ref.shape[0]
    row = lax.broadcasted_iota(jnp.int32, (height, pixels), 0)
    note = note_ref[...].astype(jnp.float32)

    @pl.loop(0, half)
    def _(j):
        line = jnp.broadcast_to(slot_ref[pl.ds(j, 1), :], (height, pixels))
        block_ref[j] = jnp.where(row == 4, line, note).astype(block_ref.dtype)

    last = pltpu.make_async_copy(
        block_ref, far_ref.at[:, pl.ds(CAP * channels, height), :], sem
    )
    last.start()

    @pl.loop(0, items)
    def _(i):
        pltpu.make_async_copy(
            source_ref.at[0], far_ref.at[0, pl.ds(0, channels), :], sem
        ).wait()

    last.wait()


def pack_rows(codes, source, note, half, span, apart):
    _, channels, pixels = source.shape
    height = note.shape[0]
    length = CAP * channels
    shapes = [(half, length + height, pixels)]
    shapes += [(length, pixels)] * half if apart else [(half, length, pixels)]
    return pl.pallas_call(
        functools.partial(pack_kernel, half, span),
        out_shape=[jax.ShapeDtypeStruct(shape, source.dtype) for shape in shapes],
        in_specs=[SMEM, VMEM, VMEM],
        out_specs=[ANY] * len(shapes),
        scratch_shapes=[
            pltpu.SMEM((SETS * half,), jnp.int32),
            pltpu.VMEM((half, pixels), jnp.float32),
            pltpu.VMEM((half, height, pixels), source.dtype),
            pltpu.SemaphoreType.DMA,
        ],
        compiler_params=pltpu.CompilerParams(vmem_limit_bytes=16 << 20),
        name="pack_rows",
    )(codes, source, note)


def split_two(values):
    high = values.astype(jnp.bfloat16)
    return high, (values - high.astype(jnp.float32)).astype(jnp.bfloat16)


def both_parts(values):
    return jnp.concatenate(split_two(values), axis=1)


def shift_left(values, offset):
    lane = lax.broadcasted_iota(jnp.int32, values.shape, 1)
    pixels = values.shape[1]
    moved = pltpu.roll(values, (-offset) % pixels, 1)
    return jnp.where((lane + offset >= 0) & (lane + offset < pixels), moved, 0.0)


def left_kernel(reference_ref, left_ref):
    rows, channels, pixels = reference_ref.shape
    i = lax.broadcasted_iota(jnp.int32, (pixels, pixels), 0)
    x = lax.broadcasted_iota(jnp.int32, (pixels, pixels), 1)
    for e in range(3):
        pick = jnp.where(x == pixels - 1 - i + (e - 1), 1.0, 0.0).astype(jnp.bfloat16)
        for r in range(rows):
            moved = lax.dot_general(
                pick,
                reference_ref[r],
                (((1,), (1,)), ((), ())),
                preferred_element_type=jnp.float32,
            )
            left_ref[r, :, e * channels : (e + 1) * channels] = moved.astype(left_ref.dtype)


def stack_left(reference):
    rows, channels, pixels = reference.shape
    return pl.pallas_call(
        left_kernel,
        out_shape=jax.ShapeDtypeStruct((rows, pixels, 3 * channels), reference.dtype),
        in_specs=[VMEM],
        out_specs=VMEM,
        compiler_params=pltpu.CompilerParams(vmem_limit_bytes=8 << 20),
        name="stack_left",
    )(reference)


def set_kernel(
    t, code_ref, note_ref, left_ref, weight_ref, edge_ref, *rest
):
    arrived_refs = rest[:-7]
    main_ref, least_ref, most_ref, stack_ref, wide_ref, total_ref, canvas_ref = rest[-7:]
    rows, channels, pixels = canvas_ref.shape
    half = note_ref.shape[0]
    lane = lax.broadcasted_iota(jnp.int32, (channels, pixels), 1)
    canvas_ref[...] = jnp.zeros_like(canvas_ref)
    owner = lax.rem(lax.axis_index("views") + t * half, SETS * half)
    counts = [0.0] * rows
    for first in (0, 2):
        named = note_ref[:, first, :].astype(jnp.float32).astype(jnp.int32) == owner
        row = lax.div(note_ref[:, first + 1, :].astype(jnp.float32).astype(jnp.int32), DSPAN)
        for r in range(rows):
            counts[r] = counts[r] + jnp.where(named & (row == r), 1.0, 0.0)
    counts = [1.0 / jnp.full((8, pixels), jnp.maximum(jnp.sum(c), 1.0)) for c in counts]

    def add_slots(home, arrived):
        for place in range(CAP):
            code = code_ref[home * (SETS * CAP) + t * CAP + place]

            @pl.when(code >= 0)
            def _():
                row = lax.div(code, DSPAN)
                begin = lax.rem(code, DSPAN)
                part = arrived[place * channels : (place + 1) * channels, :]
                moved = pltpu.roll(part.astype(jnp.float32), begin, 1)
                canvas_ref[row] = canvas_ref[row] + jnp.where(lane >= begin, moved, 0.0)

    if len(arrived_refs) > 1:
        for k, arrived_ref in enumerate(arrived_refs):
            add_slots(lax.rem(lax.axis_index("views"), half) ^ k, arrived_ref)
    else:

        @pl.loop(0, half)
        def _(home):
            add_slots(home, arrived_refs[0].at[home])

    for r in range(rows):
        mean = canvas_ref[r] * jnp.concatenate([counts[r]] * (channels // 8), axis=0)
        for e in range(3):
            stack_ref[r, e * channels : (e + 1) * channels, :] = shift_left(mean, e - 1)
        edge = jnp.broadcast_to(mean[:, :1], (channels, pixels)) * edge_ref[...]
        wide = jnp.dot(
            left_ref[r, :, 2 * channels :], both_parts(edge), preferred_element_type=jnp.float32
        )
        total_ref[(rows + 2) * 3 + r] = wide[:, :pixels] + wide[:, pixels:]

    done = set()
    for tap in range(9):
        wide_ref[...] = jnp.broadcast_to(weight_ref[:, tap : tap + 1], wide_ref.shape)
        for r in range(rows):
            right = both_parts(stack_ref[r] * wide_ref[...])
            wide = jnp.dot(left_ref[r], right, preferred_element_type=jnp.float32)
            part = wide[:, :pixels] + wide[:, pixels:]
            place = (r + 2 - tap // 3) * 3 + tap % 3
            total_ref[place] = total_ref[place] + part if place in done else part
            done.add(place)

    x = pixels - 1 - lax.broadcasted_iota(jnp.int32, (pixels, pixels), 0)
    v = lax.broadcasted_iota(jnp.int32, (pixels, pixels), 1)
    inside = (x >= v) & (x - v < DISP)
    border = (x < DISP - 1) & ((v >= pixels - 2) | (v < 1))
    for r in range(rows + 2):
        total = jnp.where(inside, total_ref[3 * r + 1], 0.0)
        for b in (0, 2):
            kept = jnp.where(inside, total_ref[3 * r + b], 0.0)
            total = total + pltpu.roll(kept, (b - 1) % pixels, 1)
        for a in range(3):
            if 0 <= r + a - 2 < rows:
                edge = total_ref[(rows + 2) * 3 + r + a - 2]
                moved = pltpu.roll(edge, (-8 * a) % pixels, 1) if a else edge
                total = total + jnp.where(border, moved, 0.0)
        total = pltpu.roll(total, 0, 1, stride=1, stride_axis=0)
        kept = total.T[pixels - DISP :]
        if r == 0:
            least_ref[0] = kept
        elif r == rows + 1:
            most_ref[0] = kept
        else:
            main_ref[r - 1] = kept


def add_set(t, codes, note, left, weight, edge, *arrived):
    rows, pixels, depth = left.shape
    channels = depth // 3
    shapes = [(n, DISP, pixels) for n in (rows, 1, 1)]
    return pl.pallas_call(
        functools.partial(set_kernel, t),
        out_shape=[jax.ShapeDtypeStruct(shape, jnp.float32) for shape in shapes],
        in_specs=[SMEM] + [VMEM] * (4 + len(arrived)),
        out_specs=[VMEM] * 3,
        scratch_shapes=[
            pltpu.VMEM((rows, depth, pixels), jnp.float32),
            pltpu.VMEM((depth, pixels), jnp.float32),
            pltpu.VMEM(((rows + 2) * 3 + rows, pixels, pixels), jnp.float32),
            pltpu.VMEM((rows, channels, pixels), jnp.float32),
        ],
        compiler_params=pltpu.CompilerParams(
            vmem_limit_bytes=(11 << 20) + sum(2 * part.size for part in arrived)
        ),
        cost_estimate=pl.CostEstimate(
            flops=2 * rows * 9 * pixels * 2 * pixels * depth,
            bytes_accessed=2 * sum(part.size for part in arrived),
            transcendentals=0,
        ),
        name="add_set",
    )(codes, note, left, weight, edge, *arrived)


def depth_kernel(own_ref, far_ref, before_ref, before_far_ref, after_ref, after_far_ref, out_ref):
    rows, pixels = out_ref.shape
    level = (DISP - 1) - lax.broadcasted_iota(jnp.int32, (DISP, pixels), 0)
    share = level.astype(jnp.float32) / DISP
    depths = []
    for r in range(rows):
        scores = own_ref[r] + far_ref[r]
        if r == 0:
            scores = scores + (before_ref[0] + before_far_ref[0])
        if r == rows - 1:
            scores = scores + (after_ref[0] + after_far_ref[0])
        weights = jnp.exp(scores - jnp.max(scores, axis=0, keepdims=True))
        bottom = jnp.sum(weights, axis=0, keepdims=True)
        depths.append(jnp.sum(weights * share, axis=0, keepdims=True) / bottom)
    lane = lax.broadcasted_iota(jnp.int32, (8, pixels), 1)
    depth = jnp.concatenate(depths + [depths[0]] * (-rows % 8), axis=0)
    out_ref[...] = jnp.take_along_axis(depth, pixels - 1 - lane, axis=1)[:rows]


def depth_rows(*parts):
    rows, _, pixels = parts[0].shape
    return pl.pallas_call(
        depth_kernel,
        out_shape=jax.ShapeDtypeStruct((rows, pixels), jnp.float32),
        in_specs=[VMEM] * len(parts),
        out_specs=VMEM,
        compiler_params=pltpu.CompilerParams(vmem_limit_bytes=4 << 20),
        name="depth_rows",
    )(*parts)


def compute(source_rows, route_owner, target_row, start_index, reference_rows, conv_weight):
    views = lax.axis_size("views")
    half = views // 2
    rows, channels, pixels = reference_rows.shape
    span = rows * DSPAN
    send = functools.partial(lax.ppermute, axis_name="views")
    home = [(i, (i + half) % views) for i in range(views)]
    groups = [list(range(half)), list(range(half, views))]
    swap = functools.partial(
        lax.all_to_all,
        axis_name="views",
        split_axis=0,
        concat_axis=0,
        tiled=True,
        axis_index_groups=groups,
    )
    owner = route_owner[:, 0]
    rest = target_row * DSPAN + start_index
    named = jnp.stack([owner, rest]).astype(jnp.bfloat16)
    named = jnp.pad(named, ((0, 0), (0, pixels - named.shape[1])), constant_values=-1)
    far_named = send(named, perm=home)
    far_rows = send(reference_rows, perm=home)
    note = jnp.pad(jnp.concatenate([named, far_named]), ((0, 12), (0, 0)))
    apart = half <= 8
    packed_far, *packed_own = pack_rows(
        owner * span + rest, source_rows, note, half, span, apart
    )
    arrived_far = swap(packed_far)
    if apart:
        arrived_own = packed_own[:1] + [None] * (half - 1)
        for k in sorted(range(1, half), key=lambda k: (k < half // 2, -k % 2, -k)):
            arrived_own[k] = send(packed_own[k], perm=[(i, i ^ k) for i in range(views)])
    else:
        arrived_own = [swap(packed_own[0])]
    note = arrived_far[:, CAP * channels :]
    codes = note[:, 4, : SETS * CAP].astype(jnp.int32).reshape(-1)

    scaled = jnp.repeat(conv_weight / CG, CG, axis=0)
    taps = scaled.transpose(3, 0, 1, 2).reshape(-1, 9)
    taps = jnp.pad(taps, ((0, 0), (0, pixels - 9)))
    edges = jnp.pad(scaled[..., 2], ((0, 0), (0, 0), (0, 5))).reshape(-1, 24)
    edges = jnp.roll(jnp.pad(edges, ((0, 0), (0, pixels - 24))), -2, 1)
    near, far = stack_left(reference_rows), stack_left(far_rows)
    far_main, far_low, far_high = add_set(1, codes, note, far, taps, edges, arrived_far)
    other_main = send(far_main, perm=home)
    other_low = send(far_low, perm=[(i, j - 1) for i, j in home if j > 0])
    other_high = send(far_high, perm=[(i, j + 1) for i, j in home if j + 1 < views])
    own_main, own_low, own_high = add_set(0, codes, note, near, taps, edges, *arrived_own)
    own_low = send(own_low, perm=[(i, i - 1) for i in range(1, views)])
    own_high = send(own_high, perm=[(i, i + 1) for i in range(views - 1)])
    return depth_rows(own_main, other_main, own_high, other_high, own_low, other_low)


def solution(mesh):
    in_specs = (
        P(("groups", "views"), None, None),
        P(("groups", "views"), None),
        P(("groups", "views")),
        P(("groups", "views")),
        P(("groups", "views"), None, None),
        P(),
    )
    out_specs = P(("groups", "views"), None)
    return jax.shard_map(compute, mesh=mesh, in_specs=in_specs, out_specs=out_specs, check_vma=False)
```

```python
import functools

import jax
import jax.numpy as jnp
from jax import lax
from jax.experimental import pallas as pl
from jax.experimental.pallas import tpu as pltpu
from jax.sharding import PartitionSpec as P


CG = 8
DISP = 96
DSPAN = 16
CAP = 2
SETS = 2
NOTE = 16

VMEM = pl.BlockSpec(memory_space=pltpu.VMEM)
SMEM = pl.BlockSpec(memory_space=pltpu.SMEM)
ANY = pl.BlockSpec(memory_space=pl.ANY)


def pack_kernel(half, apart, route_ref, target_ref, start_ref, source_ref, far_ref, *rest):
    own_refs = rest[:-3]
    slot_ref, count_ref, sem = rest[-3:]
    items, channels, pixels = source_ref.shape
    side = lax.div(lax.axis_index("views"), half)
    here = lax.rem(lax.axis_index("views"), half)
    lane = lax.broadcasted_iota(jnp.int32, (1, pixels), 1)
    slot_ref[...] = jnp.full_like(slot_ref, -1.0)

    @pl.loop(0, SETS * half)
    def _(j):
        count_ref[j] = 0

    @pl.loop(0, items)
    def _(i):
        owner = route_ref[i]
        rest = target_ref[i] * DSPAN + start_ref[i]
        home = lax.rem(owner, half)
        for t in range(SETS):

            @pl.when((lax.div(owner, half) == side) == (t == 0))
            def _():
                place = count_ref[t * half + home]
                count_ref[t * half + home] = place + 1
                first = pl.multiple_of(place * channels, channels)
                if t == 0 and apart:
                    for k, own_ref in enumerate(own_refs):

                        @pl.when(home == here ^ k)
                        def _():
                            target = own_ref.at[pl.ds(first, channels), :]
                            pltpu.make_async_copy(source_ref.at[i], target, sem).start()
                else:
                    target = (own_refs[0], far_ref)[t].at[home, pl.ds(first, channels), :]
                    pltpu.make_async_copy(source_ref.at[i], target, sem).start()
                value = jnp.full((1, pixels), rest.astype(jnp.float32))
                line = slot_ref[pl.ds(home, 1), :]
                slot_ref[pl.ds(home, 1), :] = jnp.where(lane == t * CAP + place, value, line)

    @pl.loop(0, items)
    def _(i):
        pltpu.make_async_copy(
            source_ref.at[0], far_ref.at[0, pl.ds(0, channels), :], sem
        ).wait()


def pack_rows(route, target, start, source, half, apart):
    _, channels, pixels = source.shape
    length = CAP * channels
    shapes = [(half, length + NOTE, pixels)]
    shapes += [(length, pixels)] * half if apart else [(half, length, pixels)]
    outs = [jax.ShapeDtypeStruct(shape, source.dtype) for shape in shapes]
    return pl.pallas_call(
        functools.partial(pack_kernel, half, apart),
        out_shape=outs + [jax.ShapeDtypeStruct((half, pixels), jnp.float32)],
        in_specs=[SMEM, SMEM, SMEM, VMEM],
        out_specs=[pl.BlockSpec(memory_space=pltpu.HBM)] * len(shapes) + [VMEM],
        scratch_shapes=[pltpu.SMEM((SETS * half,), jnp.int32), pltpu.SemaphoreType.DMA],
        compiler_params=pltpu.CompilerParams(vmem_limit_bytes=16 << 20),
        name="pack_rows",
    )(keep(route), keep(target), keep(start), keep(source))


def note_kernel(packed_ref, slot_ref, near_ref, far_ref, out_ref, block_ref, sem):
    half, pixels = slot_ref.shape
    fixed = [near_ref[...].astype(jnp.float32), far_ref[...].astype(jnp.float32)]
    rest = jnp.zeros((NOTE - 5, pixels), jnp.float32)

    @pl.loop(0, half)
    def _(j):
        lines = fixed + [slot_ref[pl.ds(j, 1), :], rest]
        block_ref[j] = jnp.concatenate(lines, axis=0).astype(block_ref.dtype)

    first = out_ref.shape[1] - NOTE
    copy = pltpu.make_async_copy(block_ref, out_ref.at[:, pl.ds(first, NOTE), :], sem)
    copy.start()
    copy.wait()


def add_note(packed, slots, near, far):
    return pl.pallas_call(
        note_kernel,
        out_shape=jax.ShapeDtypeStruct(packed.shape, packed.dtype),
        in_specs=[ANY, VMEM, VMEM, VMEM],
        out_specs=ANY,
        scratch_shapes=[
            pltpu.VMEM((packed.shape[0], NOTE, packed.shape[2]), packed.dtype),
            pltpu.SemaphoreType.DMA,
        ],
        input_output_aliases={0: 0},
        compiler_params=pltpu.CompilerParams(vmem_limit_bytes=4 << 20),
        name="add_note",
    )(packed, slots, near, far)


def keep(values):
    return pltpu.with_memory_space_constraint(values, pltpu.HBM)


def split_two(values):
    high = values.astype(jnp.bfloat16)
    return high, (values - high.astype(jnp.float32)).astype(jnp.bfloat16)


def both_parts(values):
    return jnp.concatenate(split_two(values), axis=1)


def shift_left(values, offset):
    lane = lax.broadcasted_iota(jnp.int32, values.shape, 1)
    pixels = values.shape[1]
    moved = pltpu.roll(values, (-offset) % pixels, 1)
    return jnp.where((lane + offset >= 0) & (lane + offset < pixels), moved, 0.0)


def left_kernel(reference_ref, left_ref):
    rows, channels, pixels = reference_ref.shape
    i = lax.broadcasted_iota(jnp.int32, (pixels, pixels), 0)
    x = lax.broadcasted_iota(jnp.int32, (pixels, pixels), 1)
    for e in range(3):
        pick = jnp.where(x == pixels - 1 - i + (e - 1), 1.0, 0.0).astype(jnp.bfloat16)
        for r in range(rows):
            moved = lax.dot_general(
                pick,
                reference_ref[r],
                (((1,), (1,)), ((), ())),
                preferred_element_type=jnp.float32,
            )
            left_ref[r, :, e * channels : (e + 1) * channels] = moved.astype(left_ref.dtype)


def stack_left(reference):
    rows, channels, pixels = reference.shape
    return pl.pallas_call(
        left_kernel,
        out_shape=jax.ShapeDtypeStruct((rows, pixels, 3 * channels), reference.dtype),
        in_specs=[VMEM],
        out_specs=VMEM,
        compiler_params=pltpu.CompilerParams(vmem_limit_bytes=8 << 20),
        name="stack_left",
    )(reference)


def set_kernel(
    t, code_ref, note_ref, left_ref, weight_ref, edge_ref, *rest
):
    arrived_refs = rest[:-11]
    main_ref, least_ref, most_ref = rest[-11:-8]
    stack_ref, wide_ref, total_ref, canvas_ref, *fetched, sems = rest[-8:]
    rows, channels, pixels = canvas_ref.shape
    fetches = [
        pltpu.make_async_copy(source, target, sems.at[n])
        for n, (source, target) in enumerate(zip((left_ref, weight_ref, edge_ref), fetched))
    ]
    for fetch in fetches:
        fetch.start()
    left_ref, weight_ref, edge_ref = fetched
    half = note_ref.shape[0]
    lane = lax.broadcasted_iota(jnp.int32, (channels, pixels), 1)
    canvas_ref[...] = jnp.zeros_like(canvas_ref)
    owner = lax.rem(lax.axis_index("views") + t * half, SETS * half)
    counts = [0.0] * rows
    for first in (0, 2):
        named = note_ref[:, first, :].astype(jnp.float32).astype(jnp.int32) == owner
        row = lax.div(note_ref[:, first + 1, :].astype(jnp.float32).astype(jnp.int32), DSPAN)
        for r in range(rows):
            counts[r] = counts[r] + jnp.where(named & (row == r), 1.0, 0.0)
    counts = [1.0 / jnp.full((8, pixels), jnp.maximum(jnp.sum(c), 1.0)) for c in counts]

    def add_slots(home, arrived):
        for place in range(CAP):
            code = code_ref[home * (SETS * CAP) + t * CAP + place]

            @pl.when(code >= 0)
            def _():
                row = lax.div(code, DSPAN)
                begin = lax.rem(code, DSPAN)
                part = arrived[place * channels : (place + 1) * channels, :]
                moved = pltpu.roll(part.astype(jnp.float32), begin, 1)
                canvas_ref[row] = canvas_ref[row] + jnp.where(lane >= begin, moved, 0.0)

    if len(arrived_refs) > 1:
        for k, arrived_ref in enumerate(arrived_refs):
            add_slots(lax.rem(lax.axis_index("views"), half) ^ k, arrived_ref)
    else:

        @pl.loop(0, half)
        def _(home):
            add_slots(home, arrived_refs[0].at[home])

    for fetch in fetches:
        fetch.wait()
    for r in range(rows):
        mean = canvas_ref[r] * jnp.concatenate([counts[r]] * (channels // 8), axis=0)
        for e in range(3):
            stack_ref[r, e * channels : (e + 1) * channels, :] = shift_left(mean, e - 1)
        edge = jnp.broadcast_to(mean[:, :1], (channels, pixels)) * edge_ref[...]
        wide = jnp.dot(
            left_ref[r, :, 2 * channels :], both_parts(edge), preferred_element_type=jnp.float32
        )
        total_ref[(rows + 2) * 3 + r] = wide[:, :pixels] + wide[:, pixels:]

    done = set()
    for tap in range(9):
        wide_ref[...] = jnp.broadcast_to(weight_ref[:, tap : tap + 1], wide_ref.shape)
        for r in range(rows):
            right = both_parts(stack_ref[r] * wide_ref[...])
            wide = jnp.dot(left_ref[r], right, preferred_element_type=jnp.float32)
            part = wide[:, :pixels] + wide[:, pixels:]
            place = (r + 2 - tap // 3) * 3 + tap % 3
            total_ref[place] = total_ref[place] + part if place in done else part
            done.add(place)

    x = pixels - 1 - lax.broadcasted_iota(jnp.int32, (pixels, pixels), 0)
    v = lax.broadcasted_iota(jnp.int32, (pixels, pixels), 1)
    inside = (x >= v) & (x - v < DISP)
    border = (x < DISP - 1) & ((v >= pixels - 2) | (v < 1))
    for r in range(rows + 2):
        total = jnp.where(inside, total_ref[3 * r + 1], 0.0)
        for b in (0, 2):
            kept = jnp.where(inside, total_ref[3 * r + b], 0.0)
            total = total + pltpu.roll(kept, (b - 1) % pixels, 1)
        for a in range(3):
            if 0 <= r + a - 2 < rows:
                edge = total_ref[(rows + 2) * 3 + r + a - 2]
                moved = pltpu.roll(edge, (-8 * a) % pixels, 1) if a else edge
                total = total + jnp.where(border, moved, 0.0)
        total = pltpu.roll(total, 0, 1, stride=1, stride_axis=0)
        kept = total.T[pixels - DISP :]
        if r == 0:
            least_ref[0] = kept
        elif r == rows + 1:
            most_ref[0] = kept
        else:
            main_ref[r - 1] = kept


def add_set(t, codes, note, left, weight, edge, *arrived):
    rows, pixels, depth = left.shape
    channels = depth // 3
    shapes = [(n, DISP, pixels) for n in (rows, 1, 1)]
    left, weight, edge = keep(left), keep(weight), keep(edge)
    return pl.pallas_call(
        functools.partial(set_kernel, t),
        out_shape=[jax.ShapeDtypeStruct(shape, jnp.float32) for shape in shapes],
        in_specs=[SMEM, VMEM, ANY, ANY, ANY] + [VMEM] * len(arrived),
        out_specs=[VMEM] * 3,
        scratch_shapes=[
            pltpu.VMEM((rows, depth, pixels), jnp.float32),
            pltpu.VMEM((depth, pixels), jnp.float32),
            pltpu.VMEM(((rows + 2) * 3 + rows, pixels, pixels), jnp.float32),
            pltpu.VMEM((rows, channels, pixels), jnp.float32),
            pltpu.VMEM(left.shape, left.dtype),
            pltpu.VMEM(weight.shape, weight.dtype),
            pltpu.VMEM(edge.shape, edge.dtype),
            pltpu.SemaphoreType.DMA((3,)),
        ],
        compiler_params=pltpu.CompilerParams(
            vmem_limit_bytes=(11 << 20) + sum(2 * part.size for part in arrived)
        ),
        cost_estimate=pl.CostEstimate(
            flops=2 * rows * 9 * pixels * 2 * pixels * depth,
            bytes_accessed=2 * sum(part.size for part in arrived),
            transcendentals=0,
        ),
        name="add_set",
    )(codes, note, left, weight, edge, *arrived)


def depth_kernel(own_ref, far_ref, before_ref, before_far_ref, after_ref, after_far_ref, out_ref):
    rows, pixels = out_ref.shape
    level = (DISP - 1) - lax.broadcasted_iota(jnp.int32, (DISP, pixels), 0)
    share = level.astype(jnp.float32) / DISP
    depths = []
    for r in range(rows):
        scores = own_ref[r] + far_ref[r]
        if r == 0:
            scores = scores + (before_ref[0] + before_far_ref[0])
        if r == rows - 1:
            scores = scores + (after_ref[0] + after_far_ref[0])
        weights = jnp.exp(scores - jnp.max(scores, axis=0, keepdims=True))
        bottom = jnp.sum(weights, axis=0, keepdims=True)
        depths.append(jnp.sum(weights * share, axis=0, keepdims=True) / bottom)
    lane = lax.broadcasted_iota(jnp.int32, (8, pixels), 1)
    depth = jnp.concatenate(depths + [depths[0]] * (-rows % 8), axis=0)
    out_ref[...] = jnp.take_along_axis(depth, pixels - 1 - lane, axis=1)[:rows]


def depth_rows(*parts):
    rows, _, pixels = parts[0].shape
    return pl.pallas_call(
        depth_kernel,
        out_shape=jax.ShapeDtypeStruct((rows, pixels), jnp.float32),
        in_specs=[VMEM] * len(parts),
        out_specs=VMEM,
        compiler_params=pltpu.CompilerParams(vmem_limit_bytes=4 << 20),
        name="depth_rows",
    )(*parts)


def compute(source_rows, route_owner, target_row, start_index, reference_rows, conv_weight):
    views = lax.axis_size("views")
    half = views // 2
    _, channels, pixels = reference_rows.shape
    send = functools.partial(lax.ppermute, axis_name="views")
    home = [(i, (i + half) % views) for i in range(views)]
    groups = [list(range(half)), list(range(half, views))]
    swap = functools.partial(
        lax.all_to_all,
        axis_name="views",
        split_axis=0,
        concat_axis=0,
        tiled=True,
        axis_index_groups=groups,
    )
    owner = route_owner[:, 0]
    rest = target_row * DSPAN + start_index
    named = jnp.stack([owner, rest]).astype(jnp.bfloat16)
    named = jnp.pad(named, ((0, 0), (0, pixels - named.shape[1])), constant_values=-1)
    far_named = send(named, perm=home)
    far_rows = send(reference_rows, perm=home)
    apart = half <= 8
    packed_far, *packed_own, slots = pack_rows(
        owner, target_row, start_index, source_rows, half, apart
    )
    packed_far = add_note(packed_far, slots, named, far_named)
    arrived_far = swap(packed_far)
    if apart:
        arrived_own = packed_own[:1] + [None] * (half - 1)
        for k in sorted(range(1, half), key=lambda k: (k < half // 2, -k % 2, -k)):
            arrived_own[k] = send(packed_own[k], perm=[(i, i ^ k) for i in range(views)])
    else:
        arrived_own = [swap(packed_own[0])]
    note = arrived_far[:, CAP * channels :]
    codes = note[:, 4, : SETS * CAP].astype(jnp.int32).reshape(-1)

    scaled = jnp.repeat(conv_weight / CG, CG, axis=0)
    taps = scaled.transpose(3, 0, 1, 2).reshape(-1, 9)
    taps = jnp.pad(taps, ((0, 0), (0, pixels - 9)))
    edges = jnp.pad(scaled[..., 2], ((0, 0), (0, 0), (0, 5))).reshape(-1, 24)
    edges = jnp.roll(jnp.pad(edges, ((0, 0), (0, pixels - 24))), -2, 1)
    near, far = stack_left(reference_rows), stack_left(far_rows)
    far_main, far_low, far_high = add_set(1, codes, note, far, taps, edges, arrived_far)
    other_main = send(far_main, perm=home)
    other_low = send(far_low, perm=[(i, j - 1) for i, j in home if j > 0])
    other_high = send(far_high, perm=[(i, j + 1) for i, j in home if j + 1 < views])
    own_main, own_low, own_high = add_set(0, codes, note, near, taps, edges, *arrived_own)
    own_low = send(own_low, perm=[(i, i - 1) for i in range(1, views)])
    own_high = send(own_high, perm=[(i, i + 1) for i in range(views - 1)])
    return depth_rows(own_main, other_main, own_high, other_high, own_low, other_low)


def solution(mesh):
    in_specs = (
        P(("groups", "views"), None, None),
        P(("groups", "views"), None),
        P(("groups", "views")),
        P(("groups", "views")),
        P(("groups", "views"), None, None),
        P(),
    )
    out_specs = P(("groups", "views"), None)
    return jax.shard_map(compute, mesh=mesh, in_specs=in_specs, out_specs=out_specs, check_vma=False)
```

```python
import functools

import jax
import jax.numpy as jnp
from jax import lax
from jax.experimental import pallas as pl
from jax.experimental.pallas import tpu as pltpu
from jax.sharding import PartitionSpec as P


CG = 8
DISP = 96
DSPAN = 16
CAP = 2
SETS = 2
NOTE = 16

VMEM = pl.BlockSpec(memory_space=pltpu.VMEM)
SMEM = pl.BlockSpec(memory_space=pltpu.SMEM)
ANY = pl.BlockSpec(memory_space=pl.ANY)


def pack_kernel(half, apart, route_ref, target_ref, start_ref, source_ref, *rest):
    packed_refs = rest[:-3]
    slot_ref, count_ref, sem = rest[-3:]
    items, channels, pixels = source_ref.shape
    side = lax.div(lax.axis_index("views"), half)
    here = lax.rem(lax.axis_index("views"), half)
    lane = lax.broadcasted_iota(jnp.int32, (1, pixels), 1)
    slot_ref[...] = jnp.full_like(slot_ref, -1.0)

    @pl.loop(0, SETS * half)
    def _(j):
        count_ref[j] = 0

    @pl.loop(0, items)
    def _(i):
        owner = route_ref[i]
        rest = target_ref[i] * DSPAN + start_ref[i]
        home = lax.rem(owner, half)
        for t in range(SETS):

            @pl.when((lax.div(owner, half) == side) == (t == 0))
            def _():
                place = count_ref[t * half + home]
                count_ref[t * half + home] = place + 1
                first = pl.multiple_of(place * channels, channels)
                if apart:
                    for k in range(half):

                        @pl.when(home == here ^ k)
                        def _():
                            target = packed_refs[(1 - t) * half + k]
                            target = target.at[pl.ds(first, channels), :]
                            pltpu.make_async_copy(source_ref.at[i], target, sem).start()
                else:
                    target = packed_refs[1 - t].at[home, pl.ds(first, channels), :]
                    pltpu.make_async_copy(source_ref.at[i], target, sem).start()
                value = jnp.full((1, pixels), rest.astype(jnp.float32))
                line = slot_ref[pl.ds(home, 1), :]
                slot_ref[pl.ds(home, 1), :] = jnp.where(lane == t * CAP + place, value, line)

    @pl.loop(0, items)
    def _(i):
        target = packed_refs[0] if apart else packed_refs[0].at[0]
        pltpu.make_async_copy(source_ref.at[0], target.at[pl.ds(0, channels), :], sem).wait()


def pack_rows(route, target, start, source, half, apart):
    _, channels, pixels = source.shape
    lengths = (CAP * channels + NOTE, CAP * channels)
    if apart:
        shapes = [(length, pixels) for length in lengths for _ in range(half)]
    else:
        shapes = [(half, length, pixels) for length in lengths]
    outs = [jax.ShapeDtypeStruct(shape, source.dtype) for shape in shapes]
    return pl.pallas_call(
        functools.partial(pack_kernel, half, apart),
        out_shape=outs + [jax.ShapeDtypeStruct((half, pixels), jnp.float32)],
        in_specs=[SMEM, SMEM, SMEM, VMEM],
        out_specs=[pl.BlockSpec(memory_space=pltpu.HBM)] * len(shapes) + [VMEM],
        scratch_shapes=[pltpu.SMEM((SETS * half,), jnp.int32), pltpu.SemaphoreType.DMA],
        compiler_params=pltpu.CompilerParams(vmem_limit_bytes=16 << 20),
        name="pack_rows",
    )(keep(route), keep(target), keep(start), keep(source))


def note_kernel(count, slot_ref, near_ref, far_ref, *rest):
    out_refs = rest[count:-2]
    block_ref, sems = rest[-2:]
    half, pixels = slot_ref.shape
    here = lax.rem(lax.axis_index("views"), half)
    fixed = [near_ref[...].astype(jnp.float32), far_ref[...].astype(jnp.float32)]
    blank = jnp.zeros((NOTE - 5, pixels), jnp.float32)
    copies = []
    for k in range(count):
        for j in [here ^ k] if count > 1 else []:
            lines = fixed + [slot_ref[pl.ds(j, 1), :], blank]
            block_ref[k] = jnp.concatenate(lines, axis=0).astype(block_ref.dtype)
            first = out_refs[k].shape[0] - NOTE
            target = out_refs[k].at[pl.ds(first, NOTE), :]
            copies.append(pltpu.make_async_copy(block_ref.at[k], target, sems.at[k]))
    if count == 1:

        @pl.loop(0, half)
        def _(j):
            lines = fixed + [slot_ref[pl.ds(j, 1), :], blank]
            block_ref[j] = jnp.concatenate(lines, axis=0).astype(block_ref.dtype)

        first = out_refs[0].shape[1] - NOTE
        target = out_refs[0].at[:, pl.ds(first, NOTE), :]
        copies.append(pltpu.make_async_copy(block_ref, target, sems.at[0]))
    for copy in copies:
        copy.start()
    for copy in copies:
        copy.wait()


def add_note(packed, slots, near, far):
    count = len(packed)
    hbm = pl.BlockSpec(memory_space=pltpu.HBM)
    return pl.pallas_call(
        functools.partial(note_kernel, count),
        out_shape=[jax.ShapeDtypeStruct(part.shape, part.dtype) for part in packed],
        in_specs=[VMEM, VMEM, VMEM] + [hbm] * count,
        out_specs=[hbm] * count,
        scratch_shapes=[
            pltpu.VMEM((slots.shape[0], NOTE, slots.shape[1]), packed[0].dtype),
            pltpu.SemaphoreType.DMA((count,)),
        ],
        input_output_aliases={3 + k: k for k in range(count)},
        compiler_params=pltpu.CompilerParams(vmem_limit_bytes=4 << 20),
        name="add_note",
    )(slots, near, far, *packed)


def keep(values):
    return pltpu.with_memory_space_constraint(values, pltpu.HBM)


def split_two(values):
    high = values.astype(jnp.bfloat16)
    return high, (values - high.astype(jnp.float32)).astype(jnp.bfloat16)


def both_parts(values):
    return jnp.concatenate(split_two(values), axis=1)


def shift_left(values, offset):
    lane = lax.broadcasted_iota(jnp.int32, values.shape, 1)
    pixels = values.shape[1]
    moved = pltpu.roll(values, (-offset) % pixels, 1)
    return jnp.where((lane + offset >= 0) & (lane + offset < pixels), moved, 0.0)


def left_kernel(reference_ref, left_ref):
    rows, channels, pixels = reference_ref.shape
    i = lax.broadcasted_iota(jnp.int32, (pixels, pixels), 0)
    x = lax.broadcasted_iota(jnp.int32, (pixels, pixels), 1)
    for e in range(3):
        pick = jnp.where(x == pixels - 1 - i + (e - 1), 1.0, 0.0).astype(jnp.bfloat16)
        for r in range(rows):
            moved = lax.dot_general(
                pick,
                reference_ref[r],
                (((1,), (1,)), ((), ())),
                preferred_element_type=jnp.float32,
            )
            left_ref[r, :, e * channels : (e + 1) * channels] = moved.astype(left_ref.dtype)


def stack_left(reference):
    rows, channels, pixels = reference.shape
    return pl.pallas_call(
        left_kernel,
        out_shape=jax.ShapeDtypeStruct((rows, pixels, 3 * channels), reference.dtype),
        in_specs=[VMEM],
        out_specs=VMEM,
        compiler_params=pltpu.CompilerParams(vmem_limit_bytes=8 << 20),
        name="stack_left",
    )(reference)


def set_kernel(
    t, code_ref, note_ref, left_ref, weight_ref, edge_ref, *rest
):
    arrived_refs = rest[:-11]
    main_ref, least_ref, most_ref = rest[-11:-8]
    stack_ref, wide_ref, total_ref, canvas_ref, *fetched, sems = rest[-8:]
    rows, channels, pixels = canvas_ref.shape
    fetches = [
        pltpu.make_async_copy(source, target, sems.at[n])
        for n, (source, target) in enumerate(zip((left_ref, weight_ref, edge_ref), fetched))
    ]
    for fetch in fetches:
        fetch.start()
    left_ref, weight_ref, edge_ref = fetched
    half = note_ref.shape[0]
    lane = lax.broadcasted_iota(jnp.int32, (channels, pixels), 1)
    canvas_ref[...] = jnp.zeros_like(canvas_ref)
    owner = lax.rem(lax.axis_index("views") + t * half, SETS * half)
    counts = [0.0] * rows
    for first in (0, 2):
        named = note_ref[:, first, :].astype(jnp.float32).astype(jnp.int32) == owner
        row = lax.div(note_ref[:, first + 1, :].astype(jnp.float32).astype(jnp.int32), DSPAN)
        for r in range(rows):
            counts[r] = counts[r] + jnp.where(named & (row == r), 1.0, 0.0)
    counts = [1.0 / jnp.full((8, pixels), jnp.maximum(jnp.sum(c), 1.0)) for c in counts]

    def add_slots(home, arrived):
        for place in range(CAP):
            code = code_ref[home * (SETS * CAP) + t * CAP + place]

            @pl.when(code >= 0)
            def _():
                row = lax.div(code, DSPAN)
                begin = lax.rem(code, DSPAN)
                part = arrived[place * channels : (place + 1) * channels, :]
                moved = pltpu.roll(part.astype(jnp.float32), begin, 1)
                canvas_ref[row] = canvas_ref[row] + jnp.where(lane >= begin, moved, 0.0)

    if len(arrived_refs) > 1:
        for k, arrived_ref in enumerate(arrived_refs):
            add_slots(k, arrived_ref)
    else:

        @pl.loop(0, half)
        def _(home):
            add_slots(home, arrived_refs[0].at[home])

    for fetch in fetches:
        fetch.wait()
    for r in range(rows):
        mean = canvas_ref[r] * jnp.concatenate([counts[r]] * (channels // 8), axis=0)
        for e in range(3):
            stack_ref[r, e * channels : (e + 1) * channels, :] = shift_left(mean, e - 1)
        edge = jnp.broadcast_to(mean[:, :1], (channels, pixels)) * edge_ref[...]
        wide = jnp.dot(
            left_ref[r, :, 2 * channels :], both_parts(edge), preferred_element_type=jnp.float32
        )
        total_ref[(rows + 2) * 3 + r] = wide[:, :pixels] + wide[:, pixels:]

    done = set()
    for tap in range(9):
        wide_ref[...] = jnp.broadcast_to(weight_ref[:, tap : tap + 1], wide_ref.shape)
        for r in range(rows):
            right = both_parts(stack_ref[r] * wide_ref[...])
            wide = jnp.dot(left_ref[r], right, preferred_element_type=jnp.float32)
            part = wide[:, :pixels] + wide[:, pixels:]
            place = (r + 2 - tap // 3) * 3 + tap % 3
            total_ref[place] = total_ref[place] + part if place in done else part
            done.add(place)

    x = pixels - 1 - lax.broadcasted_iota(jnp.int32, (pixels, pixels), 0)
    v = lax.broadcasted_iota(jnp.int32, (pixels, pixels), 1)
    inside = (x >= v) & (x - v < DISP)
    border = (x < DISP - 1) & ((v >= pixels - 2) | (v < 1))
    for r in range(rows + 2):
        total = jnp.where(inside, total_ref[3 * r + 1], 0.0)
        for b in (0, 2):
            kept = jnp.where(inside, total_ref[3 * r + b], 0.0)
            total = total + pltpu.roll(kept, (b - 1) % pixels, 1)
        for a in range(3):
            if 0 <= r + a - 2 < rows:
                edge = total_ref[(rows + 2) * 3 + r + a - 2]
                moved = pltpu.roll(edge, (-8 * a) % pixels, 1) if a else edge
                total = total + jnp.where(border, moved, 0.0)
        total = pltpu.roll(total, 0, 1, stride=1, stride_axis=0)
        kept = total.T[pixels - DISP :]
        if r == 0:
            least_ref[0] = kept
        elif r == rows + 1:
            most_ref[0] = kept
        else:
            main_ref[r - 1] = kept


def add_set(t, codes, note, left, weight, edge, *arrived):
    rows, pixels, depth = left.shape
    channels = depth // 3
    shapes = [(n, DISP, pixels) for n in (rows, 1, 1)]
    left, weight, edge = keep(left), keep(weight), keep(edge)
    return pl.pallas_call(
        functools.partial(set_kernel, t),
        out_shape=[jax.ShapeDtypeStruct(shape, jnp.float32) for shape in shapes],
        in_specs=[SMEM, VMEM, ANY, ANY, ANY] + [VMEM] * len(arrived),
        out_specs=[VMEM] * 3,
        scratch_shapes=[
            pltpu.VMEM((rows, depth, pixels), jnp.float32),
            pltpu.VMEM((depth, pixels), jnp.float32),
            pltpu.VMEM(((rows + 2) * 3 + rows, pixels, pixels), jnp.float32),
            pltpu.VMEM((rows, channels, pixels), jnp.float32),
            pltpu.VMEM(left.shape, left.dtype),
            pltpu.VMEM(weight.shape, weight.dtype),
            pltpu.VMEM(edge.shape, edge.dtype),
            pltpu.SemaphoreType.DMA((3,)),
        ],
        compiler_params=pltpu.CompilerParams(
            vmem_limit_bytes=(11 << 20) + sum(2 * part.size for part in arrived)
        ),
        cost_estimate=pl.CostEstimate(
            flops=2 * rows * 9 * pixels * 2 * pixels * depth,
            bytes_accessed=2 * sum(part.size for part in arrived),
            transcendentals=0,
        ),
        name="add_set",
    )(codes, note, left, weight, edge, *arrived)


def depth_kernel(own_ref, far_ref, before_ref, before_far_ref, after_ref, after_far_ref, out_ref):
    rows, pixels = out_ref.shape
    level = (DISP - 1) - lax.broadcasted_iota(jnp.int32, (DISP, pixels), 0)
    share = level.astype(jnp.float32) / DISP
    depths = []
    for r in range(rows):
        scores = own_ref[r] + far_ref[r]
        if r == 0:
            scores = scores + (before_ref[0] + before_far_ref[0])
        if r == rows - 1:
            scores = scores + (after_ref[0] + after_far_ref[0])
        weights = jnp.exp(scores - jnp.max(scores, axis=0, keepdims=True))
        bottom = jnp.sum(weights, axis=0, keepdims=True)
        depths.append(jnp.sum(weights * share, axis=0, keepdims=True) / bottom)
    lane = lax.broadcasted_iota(jnp.int32, (8, pixels), 1)
    depth = jnp.concatenate(depths + [depths[0]] * (-rows % 8), axis=0)
    out_ref[...] = jnp.take_along_axis(depth, pixels - 1 - lane, axis=1)[:rows]


def depth_rows(*parts):
    rows, _, pixels = parts[0].shape
    return pl.pallas_call(
        depth_kernel,
        out_shape=jax.ShapeDtypeStruct((rows, pixels), jnp.float32),
        in_specs=[VMEM] * len(parts),
        out_specs=VMEM,
        compiler_params=pltpu.CompilerParams(vmem_limit_bytes=4 << 20),
        name="depth_rows",
    )(*parts)


def compute(source_rows, route_owner, target_row, start_index, reference_rows, conv_weight):
    views = lax.axis_size("views")
    half = views // 2
    _, channels, pixels = reference_rows.shape
    send = functools.partial(lax.ppermute, axis_name="views")
    home = [(i, (i + half) % views) for i in range(views)]
    groups = [list(range(half)), list(range(half, views))]
    swap = functools.partial(
        lax.all_to_all,
        axis_name="views",
        split_axis=0,
        concat_axis=0,
        tiled=True,
        axis_index_groups=groups,
    )
    owner = route_owner[:, 0]
    rest = target_row * DSPAN + start_index
    named = jnp.stack([owner, rest]).astype(jnp.bfloat16)
    named = jnp.pad(named, ((0, 0), (0, pixels - named.shape[1])), constant_values=-1)
    far_named = send(named, perm=home)
    far_rows = send(reference_rows, perm=home)
    apart = half <= 8
    *packed, slots = pack_rows(
        owner, target_row, start_index, source_rows, half, apart
    )
    count = len(packed) // SETS
    packed_far = list(add_note(packed[:count], slots, named, far_named))
    packed_own = list(packed[count:])

    def swap_all(parts):
        if not apart:
            return [swap(parts[0])]
        arrived = parts[:1] + [None] * (half - 1)
        for k in sorted(range(1, half), key=lambda k: (k < half // 2, -k % 2, -k)):
            arrived[k] = send(parts[k], perm=[(i, i ^ k) for i in range(views)])
        return arrived

    arrived_far = swap_all(packed_far)
    arrived_own = swap_all(packed_own)
    if apart:
        note = jnp.stack([part[CAP * channels :] for part in arrived_far])
    else:
        note = arrived_far[0][:, CAP * channels :]
    codes = note[:, 4, : SETS * CAP].astype(jnp.int32).reshape(-1)

    scaled = jnp.repeat(conv_weight / CG, CG, axis=0)
    taps = scaled.transpose(3, 0, 1, 2).reshape(-1, 9)
    taps = jnp.pad(taps, ((0, 0), (0, pixels - 9)))
    edges = jnp.pad(scaled[..., 2], ((0, 0), (0, 0), (0, 5))).reshape(-1, 24)
    edges = jnp.roll(jnp.pad(edges, ((0, 0), (0, pixels - 24))), -2, 1)
    near, far = stack_left(reference_rows), stack_left(far_rows)
    far_main, far_low, far_high = add_set(1, codes, note, far, taps, edges, *arrived_far)
    other_main = send(far_main, perm=home)
    other_low = send(far_low, perm=[(i, j - 1) for i, j in home if j > 0])
    other_high = send(far_high, perm=[(i, j + 1) for i, j in home if j + 1 < views])
    own_main, own_low, own_high = add_set(0, codes, note, near, taps, edges, *arrived_own)
    own_low = send(own_low, perm=[(i, i - 1) for i in range(1, views)])
    own_high = send(own_high, perm=[(i, i + 1) for i in range(views - 1)])
    return depth_rows(own_main, other_main, own_high, other_high, own_low, other_low)


def solution(mesh):
    in_specs = (
        P(("groups", "views"), None, None),
        P(("groups", "views"), None),
        P(("groups", "views")),
        P(("groups", "views")),
        P(("groups", "views"), None, None),
        P(),
    )
    out_specs = P(("groups", "views"), None)
    return jax.shard_map(compute, mesh=mesh, in_specs=in_specs, out_specs=out_specs, check_vma=False)
```

```python
import functools

import jax
import jax.numpy as jnp
from jax import lax
from jax.experimental import pallas as pl
from jax.experimental.pallas import tpu as pltpu
from jax.sharding import PartitionSpec as P


CG = 8
DISP = 96
DSPAN = 16
CAP = 2
SETS = 2
NOTE = 16

VMEM = pl.BlockSpec(memory_space=pltpu.VMEM)
SMEM = pl.BlockSpec(memory_space=pltpu.SMEM)
ANY = pl.BlockSpec(memory_space=pl.ANY)


def pack_kernel(half, apart, route_ref, target_ref, start_ref, rows_ref, *rest):
    packed_refs = rest[:-6]
    slot_ref, count_ref, place_ref, source_ref, load_sem, sem = rest[-6:]
    items, channels, pixels = source_ref.shape
    load = pltpu.make_async_copy(rows_ref, source_ref, load_sem)
    load.start()
    side = lax.div(lax.axis_index("views"), half)
    here = lax.rem(lax.axis_index("views"), half)
    lane = lax.broadcasted_iota(jnp.int32, (1, pixels), 1)
    slot_ref[...] = jnp.full_like(slot_ref, -1.0)

    @pl.loop(0, SETS * half)
    def _(j):
        count_ref[j] = 0

    @pl.loop(0, items)
    def _(i):
        owner = route_ref[i]
        rest = target_ref[i] * DSPAN + start_ref[i]
        home = lax.rem(owner, half)
        t = lax.rem(lax.div(owner, half) + side, SETS)
        place = count_ref[t * half + home]
        count_ref[t * half + home] = place + 1
        place_ref[i] = place
        value = jnp.full((1, pixels), rest.astype(jnp.float32))
        line = slot_ref[pl.ds(home, 1), :]
        slot_ref[pl.ds(home, 1), :] = jnp.where(lane == t * CAP + place, value, line)

    load.wait()

    @pl.loop(0, items)
    def _(i):
        owner = route_ref[i]
        home = lax.rem(owner, half)
        t = lax.rem(lax.div(owner, half) + side, SETS)
        first = pl.multiple_of(place_ref[i] * channels, channels)
        if apart:
            for n, packed_ref in enumerate(packed_refs):

                @pl.when((1 - t) * half + (home ^ here) == n)
                def _():
                    target = packed_ref.at[pl.ds(first, channels), :]
                    pltpu.make_async_copy(source_ref.at[i], target, sem).start()
        else:
            for n, packed_ref in enumerate(packed_refs):

                @pl.when(1 - t == n)
                def _():
                    target = packed_ref.at[home, pl.ds(first, channels), :]
                    pltpu.make_async_copy(source_ref.at[i], target, sem).start()

    @pl.loop(0, items)
    def _(i):
        target = packed_refs[0] if apart else packed_refs[0].at[0]
        pltpu.make_async_copy(source_ref.at[0], target.at[pl.ds(0, channels), :], sem).wait()


def pack_rows(route, target, start, source, half, apart):
    items, channels, pixels = source.shape
    lengths = (CAP * channels + NOTE, CAP * channels)
    if apart:
        shapes = [(length, pixels) for length in lengths for _ in range(half)]
    else:
        shapes = [(half, length, pixels) for length in lengths]
    outs = [jax.ShapeDtypeStruct(shape, source.dtype) for shape in shapes]
    return pl.pallas_call(
        functools.partial(pack_kernel, half, apart),
        out_shape=outs + [jax.ShapeDtypeStruct((half, pixels), jnp.float32)],
        in_specs=[SMEM, SMEM, SMEM, ANY],
        out_specs=[pl.BlockSpec(memory_space=pltpu.HBM)] * len(shapes) + [VMEM],
        scratch_shapes=[
            pltpu.SMEM((SETS * half,), jnp.int32),
            pltpu.SMEM((items,), jnp.int32),
            pltpu.VMEM(source.shape, source.dtype),
            pltpu.SemaphoreType.DMA,
            pltpu.SemaphoreType.DMA,
        ],
        compiler_params=pltpu.CompilerParams(vmem_limit_bytes=16 << 20),
        name="pack_rows",
    )(keep(route), keep(target), keep(start), keep(source))


def note_kernel(count, slot_ref, near_ref, far_ref, *rest):
    out_refs = rest[count:-2]
    block_ref, sems = rest[-2:]
    half, pixels = slot_ref.shape
    here = lax.rem(lax.axis_index("views"), half)
    fixed = [near_ref[...].astype(jnp.float32), far_ref[...].astype(jnp.float32)]
    blank = jnp.zeros((NOTE - 5, pixels), jnp.float32)
    copies = []
    for k in range(count):
        for j in [here ^ k] if count > 1 else []:
            lines = fixed + [slot_ref[pl.ds(j, 1), :], blank]
            block_ref[k] = jnp.concatenate(lines, axis=0).astype(block_ref.dtype)
            first = out_refs[k].shape[0] - NOTE
            target = out_refs[k].at[pl.ds(first, NOTE), :]
            copies.append(pltpu.make_async_copy(block_ref.at[k], target, sems.at[k]))
    if count == 1:

        @pl.loop(0, half)
        def _(j):
            lines = fixed + [slot_ref[pl.ds(j, 1), :], blank]
            block_ref[j] = jnp.concatenate(lines, axis=0).astype(block_ref.dtype)

        first = out_refs[0].shape[1] - NOTE
        target = out_refs[0].at[:, pl.ds(first, NOTE), :]
        copies.append(pltpu.make_async_copy(block_ref, target, sems.at[0]))
    for copy in copies:
        copy.start()
    for copy in copies:
        copy.wait()


def add_note(packed, slots, near, far):
    count = len(packed)
    hbm = pl.BlockSpec(memory_space=pltpu.HBM)
    return pl.pallas_call(
        functools.partial(note_kernel, count),
        out_shape=[jax.ShapeDtypeStruct(part.shape, part.dtype) for part in packed],
        in_specs=[VMEM, VMEM, VMEM] + [hbm] * count,
        out_specs=[hbm] * count,
        scratch_shapes=[
            pltpu.VMEM((slots.shape[0], NOTE, slots.shape[1]), packed[0].dtype),
            pltpu.SemaphoreType.DMA((count,)),
        ],
        input_output_aliases={3 + k: k for k in range(count)},
        compiler_params=pltpu.CompilerParams(vmem_limit_bytes=4 << 20),
        name="add_note",
    )(slots, near, far, *packed)


def keep(values):
    return pltpu.with_memory_space_constraint(values, pltpu.HBM)


def split_two(values):
    high = values.astype(jnp.bfloat16)
    return high, (values - high.astype(jnp.float32)).astype(jnp.bfloat16)


def both_parts(values):
    return jnp.concatenate(split_two(values), axis=1)


def shift_left(values, offset):
    lane = lax.broadcasted_iota(jnp.int32, values.shape, 1)
    pixels = values.shape[1]
    moved = pltpu.roll(values, (-offset) % pixels, 1)
    return jnp.where((lane + offset >= 0) & (lane + offset < pixels), moved, 0.0)


def left_kernel(reference_ref, left_ref):
    rows, channels, pixels = reference_ref.shape
    i = lax.broadcasted_iota(jnp.int32, (pixels, pixels), 0)
    x = lax.broadcasted_iota(jnp.int32, (pixels, pixels), 1)
    for e in range(3):
        pick = jnp.where(x == pixels - 1 - i + (e - 1), 1.0, 0.0).astype(jnp.bfloat16)
        for r in range(rows):
            moved = lax.dot_general(
                pick,
                reference_ref[r],
                (((1,), (1,)), ((), ())),
                preferred_element_type=jnp.float32,
            )
            left_ref[r, :, e * channels : (e + 1) * channels] = moved.astype(left_ref.dtype)


def stack_left(reference):
    rows, channels, pixels = reference.shape
    return pl.pallas_call(
        left_kernel,
        out_shape=jax.ShapeDtypeStruct((rows, pixels, 3 * channels), reference.dtype),
        in_specs=[VMEM],
        out_specs=VMEM,
        compiler_params=pltpu.CompilerParams(vmem_limit_bytes=8 << 20),
        name="stack_left",
    )(reference)


def fetch_all(sources, targets, sems):
    copies = [
        pltpu.make_async_copy(source, target, sems.at[n])
        for n, (source, target) in enumerate(zip(sources, targets))
    ]
    for copy in copies:
        copy.start()
    return copies


def fill_canvas(t, code_ref, note_ref, arrived_refs, canvas_ref):
    rows, channels, pixels = canvas_ref.shape
    half = note_ref.shape[0]
    lane = lax.broadcasted_iota(jnp.int32, (channels, pixels), 1)
    canvas_ref[...] = jnp.zeros_like(canvas_ref)
    owner = lax.rem(lax.axis_index("views") + t * half, SETS * half)
    counts = [0.0] * rows
    for first in (0, 2):
        named = note_ref[:, first, :].astype(jnp.float32).astype(jnp.int32) == owner
        row = lax.div(note_ref[:, first + 1, :].astype(jnp.float32).astype(jnp.int32), DSPAN)
        for r in range(rows):
            counts[r] = counts[r] + jnp.where(named & (row == r), 1.0, 0.0)

    def add_slots(home, arrived):
        for place in range(CAP):
            code = code_ref[home * (SETS * CAP) + t * CAP + place]

            @pl.when(code >= 0)
            def _():
                row = lax.div(code, DSPAN)
                begin = lax.rem(code, DSPAN)
                part = arrived[place * channels : (place + 1) * channels, :]
                moved = pltpu.roll(part.astype(jnp.float32), begin, 1)
                canvas_ref[row] = canvas_ref[row] + jnp.where(lane >= begin, moved, 0.0)

    if len(arrived_refs) > 1:
        for k, arrived_ref in enumerate(arrived_refs):
            add_slots(k, arrived_ref)
    else:

        @pl.loop(0, half)
        def _(home):
            add_slots(home, arrived_refs[0].at[home])

    return [1.0 / jnp.full((8, pixels), jnp.maximum(jnp.sum(c), 1.0)) for c in counts]


def mean_of(canvas_ref, shares, r):
    return canvas_ref[r] * jnp.concatenate([shares[r]] * (canvas_ref.shape[1] // 8), axis=0)


def fill_stack(mean, stack):
    channels = mean.shape[0]
    for e in range(3):
        stack[e * channels : (e + 1) * channels, :] = shift_left(mean, e - 1)


def edge_dot(mean, left, edge_ref):
    channels, pixels = mean.shape
    edge = jnp.broadcast_to(mean[:, :1], (channels, pixels)) * edge_ref[...]
    last = left[:, 2 * channels :]
    wide = jnp.dot(last, both_parts(edge), preferred_element_type=jnp.float32)
    return wide[:, :pixels] + wide[:, pixels:]


def tap_dots(wanted, rows, stack_of, left_ref, weight_ref, wide_ref, total_ref):
    pixels = total_ref.shape[1]
    done = set()
    for tap in range(9):
        sources = [r for r in range(rows) if r + 2 - tap // 3 in wanted]
        if sources:
            wide_ref[...] = jnp.broadcast_to(weight_ref[:, tap : tap + 1], wide_ref.shape)
        for r in sources:
            right = both_parts(stack_of(r)[...] * wide_ref[...])
            wide = jnp.dot(left_ref[r], right, preferred_element_type=jnp.float32)
            part = wide[:, :pixels] + wide[:, pixels:]
            place = (r + 2 - tap // 3) * 3 + tap % 3
            total_ref[place] = total_ref[place] + part if place in done else part
            done.add(place)


def finish_row(row, rows, total_ref, edge_of):
    pixels = total_ref.shape[1]
    x = pixels - 1 - lax.broadcasted_iota(jnp.int32, (pixels, pixels), 0)
    v = lax.broadcasted_iota(jnp.int32, (pixels, pixels), 1)
    inside = (x >= v) & (x - v < DISP)
    border = (x < DISP - 1) & ((v >= pixels - 2) | (v < 1))
    total = jnp.where(inside, total_ref[3 * row + 1], 0.0)
    for b in (0, 2):
        kept = jnp.where(inside, total_ref[3 * row + b], 0.0)
        total = total + pltpu.roll(kept, (b - 1) % pixels, 1)
    for a in range(3):
        if 0 <= row + a - 2 < rows:
            edge = edge_of(row + a - 2)
            moved = pltpu.roll(edge, (-8 * a) % pixels, 1) if a else edge
            total = total + jnp.where(border, moved, 0.0)
    total = pltpu.roll(total, 0, 1, stride=1, stride_axis=0)
    return total.T[pixels - DISP :]


def set_kernel(t, code_ref, note_ref, left_ref, weight_ref, edge_ref, *rest):
    arrived_refs = rest[:-12]
    main_ref, least_ref, most_ref = rest[-12:-9]
    stack_ref, wide_ref, total_ref, term_ref, canvas_ref, *fetched, sems = rest[-9:]
    rows = canvas_ref.shape[0]
    copies = fetch_all((left_ref, weight_ref, edge_ref), fetched, sems)
    left_ref, weight_ref, edge_ref = fetched
    shares = fill_canvas(t, code_ref, note_ref, arrived_refs, canvas_ref)
    for copy in copies:
        copy.wait()
    for r in range(rows):
        mean = mean_of(canvas_ref, shares, r)
        fill_stack(mean, stack_ref.at[r])
        term_ref[r] = edge_dot(mean, left_ref[r], edge_ref)
    wanted = range(rows + 2)
    tap_dots(wanted, rows, lambda r: stack_ref.at[r], left_ref, weight_ref, wide_ref, total_ref)
    for row in wanted:
        kept = finish_row(row, rows, total_ref, lambda r: term_ref[r])
        if row == 0:
            least_ref[0] = kept
        elif row == rows + 1:
            most_ref[0] = kept
        else:
            main_ref[row - 1] = kept


def ends_kernel(t, code_ref, note_ref, left_ref, weight_ref, edge_ref, *rest):
    arrived_refs = rest[:-12]
    least_ref, most_ref, stack_ref, term_ref, inner_ref = rest[-12:-7]
    wide_ref, total_ref, canvas_ref, *fetched, sems = rest[-7:]
    rows = canvas_ref.shape[0]
    copies = fetch_all((left_ref, weight_ref, edge_ref), fetched, sems)
    left_ref, weight_ref, edge_ref = fetched
    shares = fill_canvas(t, code_ref, note_ref, arrived_refs, canvas_ref)
    for copy in copies:
        copy.wait()
    place = {0: 0, rows - 1: 1}
    for r in range(rows):
        mean = mean_of(canvas_ref, shares, r)
        if r in place:
            fill_stack(mean, stack_ref.at[place[r]])
            term_ref[place[r]] = edge_dot(mean, left_ref[r], edge_ref)
        else:
            inner_ref[r - 1] = mean
    stack_of = lambda r: stack_ref.at[place[r]]
    tap_dots((0, rows + 1), rows, stack_of, left_ref, weight_ref, wide_ref, total_ref)
    least_ref[0] = finish_row(0, rows, total_ref, lambda r: term_ref[place[r]])
    most_ref[0] = finish_row(rows + 1, rows, total_ref, lambda r: term_ref[place[r]])


def middle_kernel(
    ends_ref, term_ref, inner_ref, left_ref, weight_ref, edge_ref, main_ref,
    stack_ref, wide_ref, total_ref, terms_ref, *rest,
):
    *fetched, sems = rest
    rows = main_ref.shape[0]
    copies = fetch_all((left_ref, weight_ref, edge_ref), fetched, sems)
    left_ref, weight_ref, edge_ref = fetched
    for copy in copies:
        copy.wait()
    place = {0: 0, rows - 1: 1}
    for r in range(1, rows - 1):
        fill_stack(inner_ref[r - 1], stack_ref.at[r - 1])
        terms_ref[r - 1] = edge_dot(inner_ref[r - 1], left_ref[r], edge_ref)
    stack_of = lambda r: ends_ref.at[place[r]] if r in place else stack_ref.at[r - 1]
    term_of = lambda r: term_ref[place[r]] if r in place else terms_ref[r - 1]
    wanted = range(1, rows + 1)
    tap_dots(wanted, rows, stack_of, left_ref, weight_ref, wide_ref, total_ref)
    for row in wanted:
        main_ref[row - 1] = finish_row(row, rows, total_ref, term_of)


def cost_of(products, pixels, depth, arrived):
    return pl.CostEstimate(
        flops=2 * products * pixels * 2 * pixels * depth,
        bytes_accessed=2 * sum(part.size for part in arrived),
        transcendentals=0,
    )


def float_shapes(shapes):
    return [jax.ShapeDtypeStruct(shape, jnp.float32) for shape in shapes]


def fetch_scratch(fixed):
    return [pltpu.VMEM(part.shape, part.dtype) for part in fixed] + [
        pltpu.SemaphoreType.DMA((len(fixed),))
    ]


def add_set(t, codes, note, left, weight, edge, *arrived):
    rows, pixels, depth = left.shape
    fixed = [keep(left), keep(weight), keep(edge)]
    return pl.pallas_call(
        functools.partial(set_kernel, t),
        out_shape=float_shapes([(n, DISP, pixels) for n in (rows, 1, 1)]),
        in_specs=[SMEM, VMEM, ANY, ANY, ANY] + [VMEM] * len(arrived),
        out_specs=[VMEM] * 3,
        scratch_shapes=[
            pltpu.VMEM((rows, depth, pixels), jnp.float32),
            pltpu.VMEM((depth, pixels), jnp.float32),
            pltpu.VMEM(((rows + 2) * 3, pixels, pixels), jnp.float32),
            pltpu.VMEM((rows, pixels, pixels), jnp.float32),
            pltpu.VMEM((rows, depth // 3, pixels), jnp.float32),
        ]
        + fetch_scratch(fixed),
        compiler_params=pltpu.CompilerParams(
            vmem_limit_bytes=(11 << 20) + sum(2 * part.size for part in arrived)
        ),
        cost_estimate=cost_of(9 * rows, pixels, depth, arrived),
        name="add_set",
    )(codes, note, *fixed, *arrived)


def add_ends(t, codes, note, left, weight, edge, *arrived):
    rows, pixels, depth = left.shape
    channels = depth // 3
    fixed = [keep(left), keep(weight), keep(edge)]
    shapes = [(1, DISP, pixels)] * 2
    shapes += [(2, depth, pixels), (2, pixels, pixels), (rows - 2, channels, pixels)]
    return pl.pallas_call(
        functools.partial(ends_kernel, t),
        out_shape=float_shapes(shapes),
        in_specs=[SMEM, VMEM, ANY, ANY, ANY] + [VMEM] * len(arrived),
        out_specs=[VMEM] * 5,
        scratch_shapes=[
            pltpu.VMEM((depth, pixels), jnp.float32),
            pltpu.VMEM(((rows + 2) * 3, pixels, pixels), jnp.float32),
            pltpu.VMEM((rows, channels, pixels), jnp.float32),
        ]
        + fetch_scratch(fixed),
        compiler_params=pltpu.CompilerParams(
            vmem_limit_bytes=(11 << 20) + sum(2 * part.size for part in arrived)
        ),
        cost_estimate=cost_of(6, pixels, depth, arrived),
        name="add_ends",
    )(codes, note, *fixed, *arrived)


def add_middle(ends, left, weight, edge):
    rows, pixels, depth = left.shape
    fixed = [keep(left), keep(weight), keep(edge)]
    return pl.pallas_call(
        middle_kernel,
        out_shape=float_shapes([(rows, DISP, pixels)])[0],
        in_specs=[VMEM] * 3 + [ANY] * 3,
        out_specs=VMEM,
        scratch_shapes=[
            pltpu.VMEM((rows - 2, depth, pixels), jnp.float32),
            pltpu.VMEM((depth, pixels), jnp.float32),
            pltpu.VMEM(((rows + 2) * 3, pixels, pixels), jnp.float32),
            pltpu.VMEM((rows - 2, pixels, pixels), jnp.float32),
        ]
        + fetch_scratch(fixed),
        compiler_params=pltpu.CompilerParams(vmem_limit_bytes=12 << 20),
        cost_estimate=cost_of(9 * rows - 6, pixels, depth, ends),
        name="add_middle",
    )(*ends, *fixed)


def depth_kernel(own_ref, far_ref, before_ref, before_far_ref, after_ref, after_far_ref, out_ref):
    rows, pixels = out_ref.shape
    level = (DISP - 1) - lax.broadcasted_iota(jnp.int32, (DISP, pixels), 0)
    share = level.astype(jnp.float32) / DISP
    depths = []
    for r in range(rows):
        scores = own_ref[r] + far_ref[r]
        if r == 0:
            scores = scores + (before_ref[0] + before_far_ref[0])
        if r == rows - 1:
            scores = scores + (after_ref[0] + after_far_ref[0])
        weights = jnp.exp(scores - jnp.max(scores, axis=0, keepdims=True))
        bottom = jnp.sum(weights, axis=0, keepdims=True)
        depths.append(jnp.sum(weights * share, axis=0, keepdims=True) / bottom)
    lane = lax.broadcasted_iota(jnp.int32, (8, pixels), 1)
    depth = jnp.concatenate(depths + [depths[0]] * (-rows % 8), axis=0)
    out_ref[...] = jnp.take_along_axis(depth, pixels - 1 - lane, axis=1)[:rows]


def depth_rows(*parts):
    rows, _, pixels = parts[0].shape
    return pl.pallas_call(
        depth_kernel,
        out_shape=jax.ShapeDtypeStruct((rows, pixels), jnp.float32),
        in_specs=[VMEM] * len(parts),
        out_specs=VMEM,
        compiler_params=pltpu.CompilerParams(vmem_limit_bytes=4 << 20),
        name="depth_rows",
    )(*parts)


def compute(source_rows, route_owner, target_row, start_index, reference_rows, conv_weight):
    views = lax.axis_size("views")
    half = views // 2
    _, channels, pixels = reference_rows.shape
    send = functools.partial(lax.ppermute, axis_name="views")
    home = [(i, (i + half) % views) for i in range(views)]
    groups = [list(range(half)), list(range(half, views))]
    swap = functools.partial(
        lax.all_to_all,
        axis_name="views",
        split_axis=0,
        concat_axis=0,
        tiled=True,
        axis_index_groups=groups,
    )
    owner = route_owner[:, 0]
    rest = target_row * DSPAN + start_index
    named = jnp.stack([owner, rest]).astype(jnp.bfloat16)
    named = jnp.pad(named, ((0, 0), (0, pixels - named.shape[1])), constant_values=-1)
    far_named = send(named, perm=home)
    far_rows = send(reference_rows, perm=home)
    apart = half <= 8
    *packed, slots = pack_rows(
        owner, target_row, start_index, source_rows, half, apart
    )
    count = len(packed) // SETS
    packed_far = list(add_note(packed[:count], slots, named, far_named))
    packed_own = list(packed[count:])

    def swap_all(parts):
        if not apart:
            return [swap(parts[0])]
        arrived = parts[:1] + [None] * (half - 1)
        for k in sorted(range(1, half), key=lambda k: (k < half // 2, -k % 2, -k)):
            arrived[k] = send(parts[k], perm=[(i, i ^ k) for i in range(views)])
        return arrived

    arrived_far = swap_all(packed_far)
    arrived_own = swap_all(packed_own)
    if apart:
        note = jnp.stack([part[CAP * channels :] for part in arrived_far])
    else:
        note = arrived_far[0][:, CAP * channels :]
    codes = note[:, 4, : SETS * CAP].astype(jnp.int32).reshape(-1)

    scaled = jnp.repeat(conv_weight / CG, CG, axis=0)
    taps = scaled.transpose(3, 0, 1, 2).reshape(-1, 9)
    taps = jnp.pad(taps, ((0, 0), (0, pixels - 9)))
    edges = jnp.pad(scaled[..., 2], ((0, 0), (0, 0), (0, 5))).reshape(-1, 24)
    edges = jnp.roll(jnp.pad(edges, ((0, 0), (0, pixels - 24))), -2, 1)
    near, far = stack_left(reference_rows), stack_left(far_rows)
    far_main, far_low, far_high = add_set(1, codes, note, far, taps, edges, *arrived_far)
    other_main = send(far_main, perm=home)
    other_low = send(far_low, perm=[(i, j - 1) for i, j in home if j > 0])
    other_high = send(far_high, perm=[(i, j + 1) for i, j in home if j + 1 < views])
    own_low, own_high, *ends = add_ends(0, codes, note, near, taps, edges, *arrived_own)
    own_low = send(own_low, perm=[(i, i - 1) for i in range(1, views)])
    own_high = send(own_high, perm=[(i, i + 1) for i in range(views - 1)])
    own_main = add_middle(ends, near, taps, edges)
    return depth_rows(own_main, other_main, own_high, other_high, own_low, other_low)


def solution(mesh):
    in_specs = (
        P(("groups", "views"), None, None),
        P(("groups", "views"), None),
        P(("groups", "views")),
        P(("groups", "views")),
        P(("groups", "views"), None, None),
        P(),
    )
    out_specs = P(("groups", "views"), None)
    return jax.shard_map(compute, mesh=mesh, in_specs=in_specs, out_specs=out_specs, check_vma=False)
```

```python
import functools

import jax
import jax.numpy as jnp
from jax import lax
from jax.experimental import pallas as pl
from jax.experimental.pallas import tpu as pltpu
from jax.sharding import PartitionSpec as P


CG = 8
DISP = 96
DSPAN = 16
CAP = 2
SETS = 2
NOTE = 16

VMEM = pl.BlockSpec(memory_space=pltpu.VMEM)
SMEM = pl.BlockSpec(memory_space=pltpu.SMEM)
ANY = pl.BlockSpec(memory_space=pl.ANY)


def pack_kernel(half, apart, route_ref, target_ref, start_ref, rows_ref, *rest):
    packed_refs = rest[:-6]
    slot_ref, count_ref, place_ref, source_ref, load_sem, sem = rest[-6:]
    items, channels, pixels = source_ref.shape
    load = pltpu.make_async_copy(rows_ref, source_ref, load_sem)
    load.start()
    side = lax.div(lax.axis_index("views"), half)
    here = lax.rem(lax.axis_index("views"), half)
    lane = lax.broadcasted_iota(jnp.int32, (1, pixels), 1)
    slot_ref[...] = jnp.full_like(slot_ref, -1.0)

    @pl.loop(0, SETS * half)
    def _(j):
        count_ref[j] = 0
        for place in range(CAP):
            place_ref[j * CAP + place] = -1

    @pl.loop(0, items)
    def _(i):
        owner = route_ref[i]
        rest = target_ref[i] * DSPAN + start_ref[i]
        home = lax.rem(owner, half)
        t = lax.rem(lax.div(owner, half) + side, SETS)
        place = count_ref[t * half + home]
        count_ref[t * half + home] = place + 1
        output = (1 - t) * half + (home ^ here if apart else home)
        place_ref[output * CAP + place] = i
        value = jnp.full((1, pixels), rest.astype(jnp.float32))
        line = slot_ref[pl.ds(home, 1), :]
        slot_ref[pl.ds(home, 1), :] = jnp.where(lane == t * CAP + place, value, line)

    load.wait()

    def copy_slots(n, home):
        packed_ref = packed_refs[n] if apart else packed_refs[n].at[home]
        for place in range(CAP):
            i = place_ref[((n if apart else n * half + home) * CAP) + place]

            @pl.when(i >= 0)
            def _():
                target = packed_ref.at[place * channels : (place + 1) * channels, :]
                pltpu.make_async_copy(source_ref.at[i], target, sem).start()

    for n in range(len(packed_refs)):
        if apart:
            copy_slots(n, 0)
        else:
            pl.loop(0, half)(functools.partial(copy_slots, n))

    @pl.loop(0, items)
    def _(i):
        target = packed_refs[0] if apart else packed_refs[0].at[0]
        pltpu.make_async_copy(source_ref.at[0], target.at[pl.ds(0, channels), :], sem).wait()


def pack_rows(route, target, start, source, half, apart):
    _, channels, pixels = source.shape
    lengths = (CAP * channels + NOTE, CAP * channels)
    if apart:
        shapes = [(length, pixels) for length in lengths for _ in range(half)]
    else:
        shapes = [(half, length, pixels) for length in lengths]
    outs = [jax.ShapeDtypeStruct(shape, source.dtype) for shape in shapes]
    return pl.pallas_call(
        functools.partial(pack_kernel, half, apart),
        out_shape=outs + [jax.ShapeDtypeStruct((half, pixels), jnp.float32)],
        in_specs=[SMEM, SMEM, SMEM, ANY],
        out_specs=[pl.BlockSpec(memory_space=pltpu.HBM)] * len(shapes) + [VMEM],
        scratch_shapes=[
            pltpu.SMEM((SETS * half,), jnp.int32),
            pltpu.SMEM((SETS * half * CAP,), jnp.int32),
            pltpu.VMEM(source.shape, source.dtype),
            pltpu.SemaphoreType.DMA,
            pltpu.SemaphoreType.DMA,
        ],
        compiler_params=pltpu.CompilerParams(vmem_limit_bytes=16 << 20),
        name="pack_rows",
    )(keep(route), keep(target), keep(start), keep(source))


def note_kernel(count, slot_ref, near_ref, far_ref, *rest):
    out_refs = rest[count:-2]
    block_ref, sems = rest[-2:]
    half, pixels = slot_ref.shape
    here = lax.rem(lax.axis_index("views"), half)
    fixed = [near_ref[...].astype(jnp.float32), far_ref[...].astype(jnp.float32)]
    blank = jnp.zeros((NOTE - 5, pixels), jnp.float32)
    copies = []
    for k in range(count):
        for j in [here ^ k] if count > 1 else []:
            lines = fixed + [slot_ref[pl.ds(j, 1), :], blank]
            block_ref[k] = jnp.concatenate(lines, axis=0).astype(block_ref.dtype)
            first = out_refs[k].shape[0] - NOTE
            target = out_refs[k].at[pl.ds(first, NOTE), :]
            copies.append(pltpu.make_async_copy(block_ref.at[k], target, sems.at[k]))
    if count == 1:

        @pl.loop(0, half)
        def _(j):
            lines = fixed + [slot_ref[pl.ds(j, 1), :], blank]
            block_ref[j] = jnp.concatenate(lines, axis=0).astype(block_ref.dtype)

        first = out_refs[0].shape[1] - NOTE
        target = out_refs[0].at[:, pl.ds(first, NOTE), :]
        copies.append(pltpu.make_async_copy(block_ref, target, sems.at[0]))
    for copy in copies:
        copy.start()
    for copy in copies:
        copy.wait()


def add_note(packed, slots, near, far):
    count = len(packed)
    hbm = pl.BlockSpec(memory_space=pltpu.HBM)
    return pl.pallas_call(
        functools.partial(note_kernel, count),
        out_shape=[jax.ShapeDtypeStruct(part.shape, part.dtype) for part in packed],
        in_specs=[VMEM, VMEM, VMEM] + [hbm] * count,
        out_specs=[hbm] * count,
        scratch_shapes=[
            pltpu.VMEM((slots.shape[0], NOTE, slots.shape[1]), packed[0].dtype),
            pltpu.SemaphoreType.DMA((count,)),
        ],
        input_output_aliases={3 + k: k for k in range(count)},
        compiler_params=pltpu.CompilerParams(vmem_limit_bytes=4 << 20),
        name="add_note",
    )(slots, near, far, *packed)


def keep(values):
    return pltpu.with_memory_space_constraint(values, pltpu.HBM)


def split_two(values):
    high = values.astype(jnp.bfloat16)
    return high, (values - high.astype(jnp.float32)).astype(jnp.bfloat16)


def both_parts(values):
    return jnp.concatenate(split_two(values), axis=1)


def shift_left(values, offset):
    lane = lax.broadcasted_iota(jnp.int32, values.shape, 1)
    pixels = values.shape[1]
    moved = pltpu.roll(values, (-offset) % pixels, 1)
    return jnp.where((lane + offset >= 0) & (lane + offset < pixels), moved, 0.0)


def left_kernel(reference_ref, left_ref):
    rows, channels, pixels = reference_ref.shape
    i = lax.broadcasted_iota(jnp.int32, (pixels, pixels), 0)
    x = lax.broadcasted_iota(jnp.int32, (pixels, pixels), 1)
    for e in range(3):
        pick = jnp.where(x == pixels - 1 - i + (e - 1), 1.0, 0.0).astype(jnp.bfloat16)
        for r in range(rows):
            moved = lax.dot_general(
                pick,
                reference_ref[r],
                (((1,), (1,)), ((), ())),
                preferred_element_type=jnp.float32,
            )
            left_ref[r, :, e * channels : (e + 1) * channels] = moved.astype(left_ref.dtype)


def stack_left(reference):
    rows, channels, pixels = reference.shape
    return pl.pallas_call(
        left_kernel,
        out_shape=jax.ShapeDtypeStruct((rows, pixels, 3 * channels), reference.dtype),
        in_specs=[VMEM],
        out_specs=VMEM,
        compiler_params=pltpu.CompilerParams(vmem_limit_bytes=8 << 20),
        name="stack_left",
    )(reference)


def fetch_all(sources, targets, sems):
    copies = [
        pltpu.make_async_copy(source, target, sems.at[n])
        for n, (source, target) in enumerate(zip(sources, targets))
    ]
    for copy in copies:
        copy.start()
    return copies


def fill_canvas(t, code_ref, note_ref, arrived_refs, canvas_ref):
    rows, channels, pixels = canvas_ref.shape
    half = note_ref.shape[0]
    lane = lax.broadcasted_iota(jnp.int32, (channels, pixels), 1)
    canvas_ref[...] = jnp.zeros_like(canvas_ref)
    owner = lax.rem(lax.axis_index("views") + t * half, SETS * half)
    counts = [0.0] * rows
    for first in (0, 2):
        named = note_ref[:, first, :].astype(jnp.float32).astype(jnp.int32) == owner
        row = lax.div(note_ref[:, first + 1, :].astype(jnp.float32).astype(jnp.int32), DSPAN)
        for r in range(rows):
            counts[r] = counts[r] + jnp.where(named & (row == r), 1.0, 0.0)

    def add_slots(home, arrived):
        for place in range(CAP):
            code = code_ref[home * (SETS * CAP) + t * CAP + place]

            @pl.when(code >= 0)
            def _():
                row = lax.div(code, DSPAN)
                begin = lax.rem(code, DSPAN)
                part = arrived[place * channels : (place + 1) * channels, :]
                moved = pltpu.roll(part.astype(jnp.float32), begin, 1)
                canvas_ref[row] = canvas_ref[row] + jnp.where(lane >= begin, moved, 0.0)

    if len(arrived_refs) > 1:
        for k, arrived_ref in enumerate(arrived_refs):
            add_slots(k, arrived_ref)
    else:

        @pl.loop(0, half)
        def _(home):
            add_slots(home, arrived_refs[0].at[home])

    return [1.0 / jnp.full((8, pixels), jnp.maximum(jnp.sum(c), 1.0)) for c in counts]


def mean_of(canvas_ref, shares, r):
    return canvas_ref[r] * jnp.concatenate([shares[r]] * (canvas_ref.shape[1] // 8), axis=0)


def fill_stack(mean, stack):
    channels = mean.shape[0]
    for e in range(3):
        stack[e * channels : (e + 1) * channels, :] = shift_left(mean, e - 1)


def edge_dot(mean, left, edge_ref):
    channels, pixels = mean.shape
    edge = jnp.broadcast_to(mean[:, :1], (channels, pixels)) * edge_ref[...]
    last = left[:, 2 * channels :]
    wide = jnp.dot(last, both_parts(edge), preferred_element_type=jnp.float32)
    return wide[:, :pixels] + wide[:, pixels:]


def tap_dots(wanted, rows, stack_of, left_ref, weight_ref, wide_ref, total_ref):
    pixels = total_ref.shape[1]
    done = set()
    for tap in range(9):
        sources = [r for r in range(rows) if r + 2 - tap // 3 in wanted]
        if sources:
            wide_ref[...] = jnp.broadcast_to(weight_ref[:, tap : tap + 1], wide_ref.shape)
        for r in sources:
            right = both_parts(stack_of(r)[...] * wide_ref[...])
            wide = jnp.dot(left_ref[r], right, preferred_element_type=jnp.float32)
            part = wide[:, :pixels] + wide[:, pixels:]
            place = (r + 2 - tap // 3) * 3 + tap % 3
            total_ref[place] = total_ref[place] + part if place in done else part
            done.add(place)


def finish_row(row, rows, total_ref, edge_of):
    pixels = total_ref.shape[1]
    x = pixels - 1 - lax.broadcasted_iota(jnp.int32, (pixels, pixels), 0)
    v = lax.broadcasted_iota(jnp.int32, (pixels, pixels), 1)
    inside = (x >= v) & (x - v < DISP)
    border = (x < DISP - 1) & ((v >= pixels - 2) | (v < 1))
    total = jnp.where(inside, total_ref[3 * row + 1], 0.0)
    for b in (0, 2):
        kept = jnp.where(inside, total_ref[3 * row + b], 0.0)
        total = total + pltpu.roll(kept, (b - 1) % pixels, 1)
    for a in range(3):
        if 0 <= row + a - 2 < rows:
            edge = edge_of(row + a - 2)
            moved = pltpu.roll(edge, (-8 * a) % pixels, 1) if a else edge
            total = total + jnp.where(border, moved, 0.0)
    total = pltpu.roll(total, 0, 1, stride=1, stride_axis=0)
    return total.T[pixels - DISP :]


def set_kernel(t, code_ref, note_ref, left_ref, weight_ref, edge_ref, *rest):
    arrived_refs = rest[:-12]
    main_ref, least_ref, most_ref = rest[-12:-9]
    stack_ref, wide_ref, total_ref, term_ref, canvas_ref, *fetched, sems = rest[-9:]
    rows = canvas_ref.shape[0]
    copies = fetch_all((left_ref, weight_ref, edge_ref), fetched, sems)
    left_ref, weight_ref, edge_ref = fetched
    shares = fill_canvas(t, code_ref, note_ref, arrived_refs, canvas_ref)
    for copy in copies:
        copy.wait()
    for r in range(rows):
        mean = mean_of(canvas_ref, shares, r)
        fill_stack(mean, stack_ref.at[r])
        term_ref[r] = edge_dot(mean, left_ref[r], edge_ref)
    wanted = range(rows + 2)
    tap_dots(wanted, rows, lambda r: stack_ref.at[r], left_ref, weight_ref, wide_ref, total_ref)
    for row in wanted:
        kept = finish_row(row, rows, total_ref, lambda r: term_ref[r])
        if row == 0:
            least_ref[0] = kept
        elif row == rows + 1:
            most_ref[0] = kept
        else:
            main_ref[row - 1] = kept


def ends_kernel(t, code_ref, note_ref, left_ref, weight_ref, edge_ref, *rest):
    arrived_refs = rest[:-12]
    least_ref, most_ref, stack_ref, term_ref, inner_ref = rest[-12:-7]
    wide_ref, total_ref, canvas_ref, *fetched, sems = rest[-7:]
    rows = canvas_ref.shape[0]
    copies = fetch_all((left_ref, weight_ref, edge_ref), fetched, sems)
    left_ref, weight_ref, edge_ref = fetched
    shares = fill_canvas(t, code_ref, note_ref, arrived_refs, canvas_ref)
    for copy in copies:
        copy.wait()
    place = {0: 0, rows - 1: 1}
    for r in range(rows):
        mean = mean_of(canvas_ref, shares, r)
        if r in place:
            fill_stack(mean, stack_ref.at[place[r]])
            term_ref[place[r]] = edge_dot(mean, left_ref[r], edge_ref)
        else:
            inner_ref[r - 1] = mean
    stack_of = lambda r: stack_ref.at[place[r]]
    tap_dots((0, rows + 1), rows, stack_of, left_ref, weight_ref, wide_ref, total_ref)
    least_ref[0] = finish_row(0, rows, total_ref, lambda r: term_ref[place[r]])
    most_ref[0] = finish_row(rows + 1, rows, total_ref, lambda r: term_ref[place[r]])


def middle_kernel(
    ends_ref, term_ref, inner_ref, left_ref, weight_ref, edge_ref, main_ref,
    stack_ref, wide_ref, total_ref, terms_ref, *rest,
):
    *fetched, sems = rest
    rows = main_ref.shape[0]
    copies = fetch_all((left_ref, weight_ref, edge_ref), fetched, sems)
    left_ref, weight_ref, edge_ref = fetched
    for copy in copies:
        copy.wait()
    place = {0: 0, rows - 1: 1}
    for r in range(1, rows - 1):
        fill_stack(inner_ref[r - 1], stack_ref.at[r - 1])
        terms_ref[r - 1] = edge_dot(inner_ref[r - 1], left_ref[r], edge_ref)
    stack_of = lambda r: ends_ref.at[place[r]] if r in place else stack_ref.at[r - 1]
    term_of = lambda r: term_ref[place[r]] if r in place else terms_ref[r - 1]
    wanted = range(1, rows + 1)
    tap_dots(wanted, rows, stack_of, left_ref, weight_ref, wide_ref, total_ref)
    for row in wanted:
        main_ref[row - 1] = finish_row(row, rows, total_ref, term_of)


def cost_of(products, pixels, depth, arrived):
    return pl.CostEstimate(
        flops=2 * products * pixels * 2 * pixels * depth,
        bytes_accessed=2 * sum(part.size for part in arrived),
        transcendentals=0,
    )


def float_shapes(shapes):
    return [jax.ShapeDtypeStruct(shape, jnp.float32) for shape in shapes]


def fetch_scratch(fixed):
    return [pltpu.VMEM(part.shape, part.dtype) for part in fixed] + [
        pltpu.SemaphoreType.DMA((len(fixed),))
    ]


def add_set(t, codes, note, left, weight, edge, *arrived):
    rows, pixels, depth = left.shape
    fixed = [keep(left), keep(weight), keep(edge)]
    return pl.pallas_call(
        functools.partial(set_kernel, t),
        out_shape=float_shapes([(n, DISP, pixels) for n in (rows, 1, 1)]),
        in_specs=[SMEM, VMEM, ANY, ANY, ANY] + [VMEM] * len(arrived),
        out_specs=[VMEM] * 3,
        scratch_shapes=[
            pltpu.VMEM((rows, depth, pixels), jnp.float32),
            pltpu.VMEM((depth, pixels), jnp.float32),
            pltpu.VMEM(((rows + 2) * 3, pixels, pixels), jnp.float32),
            pltpu.VMEM((rows, pixels, pixels), jnp.float32),
            pltpu.VMEM((rows, depth // 3, pixels), jnp.float32),
        ]
        + fetch_scratch(fixed),
        compiler_params=pltpu.CompilerParams(
            vmem_limit_bytes=(11 << 20) + sum(2 * part.size for part in arrived)
        ),
        cost_estimate=cost_of(9 * rows, pixels, depth, arrived),
        name="add_set",
    )(codes, note, *fixed, *arrived)


def add_ends(t, codes, note, left, weight, edge, *arrived):
    rows, pixels, depth = left.shape
    channels = depth // 3
    fixed = [keep(left), keep(weight), keep(edge)]
    shapes = [(1, DISP, pixels)] * 2
    shapes += [(2, depth, pixels), (2, pixels, pixels), (rows - 2, channels, pixels)]
    return pl.pallas_call(
        functools.partial(ends_kernel, t),
        out_shape=float_shapes(shapes),
        in_specs=[SMEM, VMEM, ANY, ANY, ANY] + [VMEM] * len(arrived),
        out_specs=[VMEM] * 5,
        scratch_shapes=[
            pltpu.VMEM((depth, pixels), jnp.float32),
            pltpu.VMEM(((rows + 2) * 3, pixels, pixels), jnp.float32),
            pltpu.VMEM((rows, channels, pixels), jnp.float32),
        ]
        + fetch_scratch(fixed),
        compiler_params=pltpu.CompilerParams(
            vmem_limit_bytes=(11 << 20) + sum(2 * part.size for part in arrived)
        ),
        cost_estimate=cost_of(6, pixels, depth, arrived),
        name="add_ends",
    )(codes, note, *fixed, *arrived)


def add_middle(ends, left, weight, edge):
    rows, pixels, depth = left.shape
    fixed = [keep(left), keep(weight), keep(edge)]
    return pl.pallas_call(
        middle_kernel,
        out_shape=float_shapes([(rows, DISP, pixels)])[0],
        in_specs=[VMEM] * 3 + [ANY] * 3,
        out_specs=VMEM,
        scratch_shapes=[
            pltpu.VMEM((rows - 2, depth, pixels), jnp.float32),
            pltpu.VMEM((depth, pixels), jnp.float32),
            pltpu.VMEM(((rows + 2) * 3, pixels, pixels), jnp.float32),
            pltpu.VMEM((rows - 2, pixels, pixels), jnp.float32),
        ]
        + fetch_scratch(fixed),
        compiler_params=pltpu.CompilerParams(vmem_limit_bytes=12 << 20),
        cost_estimate=cost_of(9 * rows - 6, pixels, depth, ends),
        name="add_middle",
    )(*ends, *fixed)


def depth_kernel(own_ref, far_ref, before_ref, before_far_ref, after_ref, after_far_ref, out_ref):
    rows, pixels = out_ref.shape
    level = (DISP - 1) - lax.broadcasted_iota(jnp.int32, (DISP, pixels), 0)
    share = level.astype(jnp.float32) / DISP
    depths = []
    for r in range(rows):
        scores = own_ref[r] + far_ref[r]
        if r == 0:
            scores = scores + (before_ref[0] + before_far_ref[0])
        if r == rows - 1:
            scores = scores + (after_ref[0] + after_far_ref[0])
        weights = jnp.exp(scores - jnp.max(scores, axis=0, keepdims=True))
        bottom = jnp.sum(weights, axis=0, keepdims=True)
        depths.append(jnp.sum(weights * share, axis=0, keepdims=True) / bottom)
    lane = lax.broadcasted_iota(jnp.int32, (8, pixels), 1)
    depth = jnp.concatenate(depths + [depths[0]] * (-rows % 8), axis=0)
    out_ref[...] = jnp.take_along_axis(depth, pixels - 1 - lane, axis=1)[:rows]


def depth_rows(*parts):
    rows, _, pixels = parts[0].shape
    return pl.pallas_call(
        depth_kernel,
        out_shape=jax.ShapeDtypeStruct((rows, pixels), jnp.float32),
        in_specs=[VMEM] * len(parts),
        out_specs=VMEM,
        compiler_params=pltpu.CompilerParams(vmem_limit_bytes=4 << 20),
        name="depth_rows",
    )(*parts)


def compute(source_rows, route_owner, target_row, start_index, reference_rows, conv_weight):
    views = lax.axis_size("views")
    half = views // 2
    _, channels, pixels = reference_rows.shape
    send = functools.partial(lax.ppermute, axis_name="views")
    home = [(i, (i + half) % views) for i in range(views)]
    groups = [list(range(half)), list(range(half, views))]
    swap = functools.partial(
        lax.all_to_all,
        axis_name="views",
        split_axis=0,
        concat_axis=0,
        tiled=True,
        axis_index_groups=groups,
    )
    owner = route_owner[:, 0]
    rest = target_row * DSPAN + start_index
    named = jnp.stack([owner, rest]).astype(jnp.bfloat16)
    named = jnp.pad(named, ((0, 0), (0, pixels - named.shape[1])), constant_values=-1)
    far_named = send(named, perm=home)
    far_rows = send(reference_rows, perm=home)
    apart = half <= 8
    *packed, slots = pack_rows(
        owner, target_row, start_index, source_rows, half, apart
    )
    count = len(packed) // SETS
    packed_far = list(add_note(packed[:count], slots, named, far_named))
    packed_own = list(packed[count:])

    def swap_all(parts):
        if not apart:
            return [swap(parts[0])]
        arrived = parts[:1] + [None] * (half - 1)
        for k in sorted(range(1, half), key=lambda k: (k < half // 2, -k % 2, -k)):
            arrived[k] = send(parts[k], perm=[(i, i ^ k) for i in range(views)])
        return arrived

    arrived_far = swap_all(packed_far)
    arrived_own = swap_all(packed_own)
    if apart:
        note = jnp.stack([part[CAP * channels :] for part in arrived_far])
    else:
        note = arrived_far[0][:, CAP * channels :]
    codes = note[:, 4, : SETS * CAP].astype(jnp.int32).reshape(-1)

    scaled = jnp.repeat(conv_weight / CG, CG, axis=0)
    taps = scaled.transpose(3, 0, 1, 2).reshape(-1, 9)
    taps = jnp.pad(taps, ((0, 0), (0, pixels - 9)))
    edges = jnp.pad(scaled[..., 2], ((0, 0), (0, 0), (0, 5))).reshape(-1, 24)
    edges = jnp.roll(jnp.pad(edges, ((0, 0), (0, pixels - 24))), -2, 1)
    near, far = stack_left(keep(reference_rows)), stack_left(far_rows)
    far_main, far_low, far_high = add_set(1, codes, note, far, taps, edges, *arrived_far)
    other_main = send(far_main, perm=home)
    other_low = send(far_low, perm=[(i, j - 1) for i, j in home if j > 0])
    other_high = send(far_high, perm=[(i, j + 1) for i, j in home if j + 1 < views])
    own_low, own_high, *ends = add_ends(0, codes, note, near, taps, edges, *arrived_own)
    own_low = send(own_low, perm=[(i, i - 1) for i in range(1, views)])
    own_high = send(own_high, perm=[(i, i + 1) for i in range(views - 1)])
    own_main = add_middle(ends, near, taps, edges)
    return depth_rows(own_main, other_main, own_high, other_high, own_low, other_low)


def solution(mesh):
    in_specs = (
        P(("groups", "views"), None, None),
        P(("groups", "views"), None),
        P(("groups", "views")),
        P(("groups", "views")),
        P(("groups", "views"), None, None),
        P(),
    )
    out_specs = P(("groups", "views"), None)
    return jax.shard_map(compute, mesh=mesh, in_specs=in_specs, out_specs=out_specs, check_vma=False)
```

```python
import functools

import jax
import jax.numpy as jnp
from jax import lax
from jax.experimental import pallas as pl
from jax.experimental.pallas import tpu as pltpu
from jax.sharding import PartitionSpec as P


CG = 8
DISP = 96
DSPAN = 16
CAP = 2
SETS = 2
NOTE = 16
GRANT = 11 << 20

VMEM = pl.BlockSpec(memory_space=pltpu.VMEM)
SMEM = pl.BlockSpec(memory_space=pltpu.SMEM)
ANY = pl.BlockSpec(memory_space=pl.ANY)


def pack_kernel(half, apart, route_ref, target_ref, start_ref, rows_ref, *rest):
    packed_refs = rest[:-6]
    slot_ref, count_ref, place_ref, source_ref, load_sem, sem = rest[-6:]
    items, channels, pixels = source_ref.shape
    load = pltpu.make_async_copy(rows_ref, source_ref, load_sem)
    load.start()
    side = lax.div(lax.axis_index("views"), half)
    here = lax.rem(lax.axis_index("views"), half)
    lane = lax.broadcasted_iota(jnp.int32, (1, pixels), 1)
    slot_ref[...] = jnp.full_like(slot_ref, -1.0)

    @pl.loop(0, SETS * half)
    def _(j):
        count_ref[j] = 0
        for place in range(CAP):
            place_ref[j * CAP + place] = -1

    @pl.loop(0, items)
    def _(i):
        owner = route_ref[i]
        rest = target_ref[i] * DSPAN + start_ref[i]
        home = lax.rem(owner, half)
        t = lax.rem(lax.div(owner, half) + side, SETS)
        place = count_ref[t * half + home]
        count_ref[t * half + home] = place + 1
        output = (1 - t) * half + (home ^ here if apart else home)
        place_ref[output * CAP + place] = i
        value = jnp.full((1, pixels), rest.astype(jnp.float32))
        line = slot_ref[pl.ds(home, 1), :]
        slot_ref[pl.ds(home, 1), :] = jnp.where(lane == t * CAP + place, value, line)

    load.wait()

    def copy_slots(n, home):
        packed_ref = packed_refs[n] if apart else packed_refs[n].at[home]
        for place in range(CAP):
            i = place_ref[((n if apart else n * half + home) * CAP) + place]

            @pl.when(i >= 0)
            def _():
                target = packed_ref.at[place * channels : (place + 1) * channels, :]
                pltpu.make_async_copy(source_ref.at[i], target, sem).start()

    for n in range(len(packed_refs)):
        if apart:
            copy_slots(n, 0)
        else:
            pl.loop(0, half)(functools.partial(copy_slots, n))

    @pl.loop(0, items)
    def _(i):
        target = packed_refs[0] if apart else packed_refs[0].at[0]
        pltpu.make_async_copy(source_ref.at[0], target.at[pl.ds(0, channels), :], sem).wait()


def pack_rows(route, target, start, source, half, apart):
    _, channels, pixels = source.shape
    lengths = (CAP * channels + NOTE, CAP * channels)
    if apart:
        shapes = [(length, pixels) for length in lengths for _ in range(half)]
    else:
        shapes = [(half, length, pixels) for length in lengths]
    outs = [jax.ShapeDtypeStruct(shape, source.dtype) for shape in shapes]
    return pl.pallas_call(
        functools.partial(pack_kernel, half, apart),
        out_shape=outs + [jax.ShapeDtypeStruct((half, pixels), jnp.float32)],
        in_specs=[SMEM, SMEM, SMEM, ANY],
        out_specs=[pl.BlockSpec(memory_space=pltpu.HBM)] * len(shapes) + [VMEM],
        scratch_shapes=[
            pltpu.SMEM((SETS * half,), jnp.int32),
            pltpu.SMEM((SETS * half * CAP,), jnp.int32),
            pltpu.VMEM(source.shape, source.dtype),
            pltpu.SemaphoreType.DMA,
            pltpu.SemaphoreType.DMA,
        ],
        compiler_params=pltpu.CompilerParams(vmem_limit_bytes=58 << 20),
        name="pack_rows",
    )(keep(route), keep(target), keep(start), keep(source))


def note_kernel(count, slot_ref, near_ref, far_ref, *rest):
    out_refs = rest[count:-2]
    block_ref, sems = rest[-2:]
    half, pixels = slot_ref.shape
    here = lax.rem(lax.axis_index("views"), half)
    fixed = [near_ref[...].astype(jnp.float32), far_ref[...].astype(jnp.float32)]
    blank = jnp.zeros((NOTE - 5, pixels), jnp.float32)
    copies = []
    for k in range(count):
        for j in [here ^ k] if count > 1 else []:
            lines = fixed + [slot_ref[pl.ds(j, 1), :], blank]
            block_ref[k] = jnp.concatenate(lines, axis=0).astype(block_ref.dtype)
            first = out_refs[k].shape[0] - NOTE
            target = out_refs[k].at[pl.ds(first, NOTE), :]
            copies.append(pltpu.make_async_copy(block_ref.at[k], target, sems.at[k]))
    if count == 1:

        @pl.loop(0, half)
        def _(j):
            lines = fixed + [slot_ref[pl.ds(j, 1), :], blank]
            block_ref[j] = jnp.concatenate(lines, axis=0).astype(block_ref.dtype)

        first = out_refs[0].shape[1] - NOTE
        target = out_refs[0].at[:, pl.ds(first, NOTE), :]
        copies.append(pltpu.make_async_copy(block_ref, target, sems.at[0]))
    for copy in copies:
        copy.start()
    for copy in copies:
        copy.wait()


def add_note(packed, slots, near, far):
    count = len(packed)
    hbm = pl.BlockSpec(memory_space=pltpu.HBM)
    return pl.pallas_call(
        functools.partial(note_kernel, count),
        out_shape=[jax.ShapeDtypeStruct(part.shape, part.dtype) for part in packed],
        in_specs=[VMEM, VMEM, VMEM] + [hbm] * count,
        out_specs=[hbm] * count,
        scratch_shapes=[
            pltpu.VMEM((slots.shape[0], NOTE, slots.shape[1]), packed[0].dtype),
            pltpu.SemaphoreType.DMA((count,)),
        ],
        input_output_aliases={3 + k: k for k in range(count)},
        compiler_params=pltpu.CompilerParams(vmem_limit_bytes=58 << 20),
        name="add_note",
    )(slots, near, far, *packed)


def keep(values):
    return pltpu.with_memory_space_constraint(values, pltpu.HBM)


def split_two(values):
    high = values.astype(jnp.bfloat16)
    return high, (values - high.astype(jnp.float32)).astype(jnp.bfloat16)


def both_parts(values):
    return jnp.concatenate(split_two(values), axis=1)


def shift_left(values, offset):
    lane = lax.broadcasted_iota(jnp.int32, values.shape, 1)
    pixels = values.shape[1]
    moved = pltpu.roll(values, (-offset) % pixels, 1)
    return jnp.where((lane + offset >= 0) & (lane + offset < pixels), moved, 0.0)


def left_kernel(reference_ref, left_ref):
    rows, channels, pixels = reference_ref.shape
    i = lax.broadcasted_iota(jnp.int32, (pixels, pixels), 0)
    x = lax.broadcasted_iota(jnp.int32, (pixels, pixels), 1)
    for e in range(3):
        pick = jnp.where(x == pixels - 1 - i + (e - 1), 1.0, 0.0).astype(jnp.bfloat16)
        for r in range(rows):
            moved = lax.dot_general(
                pick,
                reference_ref[r],
                (((1,), (1,)), ((), ())),
                preferred_element_type=jnp.float32,
            )
            left_ref[r, :, e * channels : (e + 1) * channels] = moved.astype(left_ref.dtype)


def stack_left(reference):
    rows, channels, pixels = reference.shape
    return pl.pallas_call(
        left_kernel,
        out_shape=jax.ShapeDtypeStruct((rows, pixels, 3 * channels), reference.dtype),
        in_specs=[VMEM],
        out_specs=VMEM,
        compiler_params=pltpu.CompilerParams(vmem_limit_bytes=8 << 20),
        name="stack_left",
    )(reference)


def fetch_all(sources, targets, sems):
    copies = [
        pltpu.make_async_copy(source, target, sems.at[n])
        for n, (source, target) in enumerate(zip(sources, targets))
    ]
    for copy in copies:
        copy.start()
    return copies


def fill_canvas(t, code_ref, note_ref, arrived_refs, canvas_ref):
    rows, channels, pixels = canvas_ref.shape
    half = note_ref.shape[0]
    lane = lax.broadcasted_iota(jnp.int32, (channels, pixels), 1)
    canvas_ref[...] = jnp.zeros_like(canvas_ref)
    owner = lax.rem(lax.axis_index("views") + t * half, SETS * half)
    counts = [0.0] * rows
    for first in (0, 2):
        named = note_ref[:, first, :].astype(jnp.float32).astype(jnp.int32) == owner
        row = lax.div(note_ref[:, first + 1, :].astype(jnp.float32).astype(jnp.int32), DSPAN)
        for r in range(rows):
            counts[r] = counts[r] + jnp.where(named & (row == r), 1.0, 0.0)

    def add_slots(home, arrived):
        for place in range(CAP):
            code = code_ref[home * (SETS * CAP) + t * CAP + place]

            @pl.when(code >= 0)
            def _():
                row = lax.div(code, DSPAN)
                begin = lax.rem(code, DSPAN)
                part = arrived[place * channels : (place + 1) * channels, :]
                moved = pltpu.roll(part.astype(jnp.float32), begin, 1)
                canvas_ref[row] = canvas_ref[row] + jnp.where(lane >= begin, moved, 0.0)

    if len(arrived_refs) > 1:
        for k, arrived_ref in enumerate(arrived_refs):
            add_slots(k, arrived_ref)
    else:

        @pl.loop(0, half)
        def _(home):
            add_slots(home, arrived_refs[0].at[home])

    return [1.0 / jnp.full((8, pixels), jnp.maximum(jnp.sum(c), 1.0)) for c in counts]


def mean_of(canvas_ref, shares, r):
    return canvas_ref[r] * jnp.concatenate([shares[r]] * (canvas_ref.shape[1] // 8), axis=0)


def fill_stack(mean, stack):
    channels = mean.shape[0]
    for e in range(3):
        stack[e * channels : (e + 1) * channels, :] = shift_left(mean, e - 1)


def edge_dot(mean, left, edge_ref):
    channels, pixels = mean.shape
    edge = jnp.broadcast_to(mean[:, :1], (channels, pixels)) * edge_ref[...]
    last = left[:, 2 * channels :]
    wide = jnp.dot(last, both_parts(edge), preferred_element_type=jnp.float32)
    return wide[:, :pixels] + wide[:, pixels:]


def tap_dots(wanted, rows, stack_of, left_ref, weight_ref, wide_ref, total_ref):
    pixels = total_ref.shape[1]
    done = set()
    for tap in range(9):
        sources = [r for r in range(rows) if r + 2 - tap // 3 in wanted]
        if sources:
            wide_ref[...] = jnp.broadcast_to(weight_ref[:, tap : tap + 1], wide_ref.shape)
        for r in sources:
            right = both_parts(stack_of(r)[...] * wide_ref[...])
            wide = jnp.dot(left_ref[r], right, preferred_element_type=jnp.float32)
            part = wide[:, :pixels] + wide[:, pixels:]
            place = (r + 2 - tap // 3) * 3 + tap % 3
            total_ref[place] = total_ref[place] + part if place in done else part
            done.add(place)


def finish_row(row, rows, total_ref, edge_of):
    pixels = total_ref.shape[1]
    x = pixels - 1 - lax.broadcasted_iota(jnp.int32, (pixels, pixels), 0)
    v = lax.broadcasted_iota(jnp.int32, (pixels, pixels), 1)
    inside = (x >= v) & (x - v < DISP)
    border = (x < DISP - 1) & ((v >= pixels - 2) | (v < 1))
    total = jnp.where(inside, total_ref[3 * row + 1], 0.0)
    for b in (0, 2):
        kept = jnp.where(inside, total_ref[3 * row + b], 0.0)
        total = total + pltpu.roll(kept, (b - 1) % pixels, 1)
    for a in range(3):
        if 0 <= row + a - 2 < rows:
            edge = edge_of(row + a - 2)
            moved = pltpu.roll(edge, (-8 * a) % pixels, 1) if a else edge
            total = total + jnp.where(border, moved, 0.0)
    total = pltpu.roll(total, 0, 1, stride=1, stride_axis=0)
    return total.T[pixels - DISP :]


def set_kernel(t, code_ref, note_ref, left_ref, weight_ref, edge_ref, *rest):
    arrived_refs = rest[:-12]
    main_ref, least_ref, most_ref = rest[-12:-9]
    stack_ref, wide_ref, total_ref, term_ref, canvas_ref, *fetched, sems = rest[-9:]
    rows = canvas_ref.shape[0]
    copies = fetch_all((left_ref, weight_ref, edge_ref), fetched, sems)
    left_ref, weight_ref, edge_ref = fetched
    shares = fill_canvas(t, code_ref, note_ref, arrived_refs, canvas_ref)
    for copy in copies:
        copy.wait()
    for r in range(rows):
        mean = mean_of(canvas_ref, shares, r)
        fill_stack(mean, stack_ref.at[r])
        term_ref[r] = edge_dot(mean, left_ref[r], edge_ref)
    wanted = range(rows + 2)
    tap_dots(wanted, rows, lambda r: stack_ref.at[r], left_ref, weight_ref, wide_ref, total_ref)
    for row in wanted:
        kept = finish_row(row, rows, total_ref, lambda r: term_ref[r])
        if row == 0:
            least_ref[0] = kept
        elif row == rows + 1:
            most_ref[0] = kept
        else:
            main_ref[row - 1] = kept


def ends_kernel(t, code_ref, note_ref, left_ref, weight_ref, edge_ref, *rest):
    arrived_refs = rest[:-12]
    least_ref, most_ref, stack_ref, term_ref, inner_ref = rest[-12:-7]
    wide_ref, total_ref, canvas_ref, *fetched, sems = rest[-7:]
    rows = canvas_ref.shape[0]
    copies = fetch_all((left_ref, weight_ref, edge_ref), fetched, sems)
    left_ref, weight_ref, edge_ref = fetched
    shares = fill_canvas(t, code_ref, note_ref, arrived_refs, canvas_ref)
    for copy in copies:
        copy.wait()
    place = {0: 0, rows - 1: 1}
    for r in range(rows):
        mean = mean_of(canvas_ref, shares, r)
        if r in place:
            fill_stack(mean, stack_ref.at[place[r]])
            term_ref[place[r]] = edge_dot(mean, left_ref[r], edge_ref)
        else:
            inner_ref[r - 1] = mean
    stack_of = lambda r: stack_ref.at[place[r]]
    tap_dots((0, rows + 1), rows, stack_of, left_ref, weight_ref, wide_ref, total_ref)
    least_ref[0] = finish_row(0, rows, total_ref, lambda r: term_ref[place[r]])
    most_ref[0] = finish_row(rows + 1, rows, total_ref, lambda r: term_ref[place[r]])


def middle_kernel(
    ends_ref, term_ref, inner_ref, left_ref, weight_ref, edge_ref, main_ref,
    stack_ref, wide_ref, total_ref, terms_ref,
):
    rows = main_ref.shape[0]
    place = {0: 0, rows - 1: 1}
    for r in range(1, rows - 1):
        fill_stack(inner_ref[r - 1], stack_ref.at[r - 1])
        terms_ref[r - 1] = edge_dot(inner_ref[r - 1], left_ref[r], edge_ref)
    stack_of = lambda r: ends_ref.at[place[r]] if r in place else stack_ref.at[r - 1]
    term_of = lambda r: term_ref[place[r]] if r in place else terms_ref[r - 1]
    wanted = range(1, rows + 1)
    tap_dots(wanted, rows, stack_of, left_ref, weight_ref, wide_ref, total_ref)
    for row in wanted:
        main_ref[row - 1] = finish_row(row, rows, total_ref, term_of)


def cost_of(products, pixels, depth, arrived):
    return pl.CostEstimate(
        flops=2 * products * pixels * 2 * pixels * depth,
        bytes_accessed=2 * sum(part.size for part in arrived),
        transcendentals=0,
    )


def float_shapes(shapes):
    return [jax.ShapeDtypeStruct(shape, jnp.float32) for shape in shapes]


def fetch_scratch(fixed):
    return [pltpu.VMEM(part.shape, part.dtype) for part in fixed] + [
        pltpu.SemaphoreType.DMA((len(fixed),))
    ]


def add_set(t, codes, note, left, weight, edge, *arrived):
    rows, pixels, depth = left.shape
    fixed = [keep(left), keep(weight), keep(edge)]
    return pl.pallas_call(
        functools.partial(set_kernel, t),
        out_shape=float_shapes([(n, DISP, pixels) for n in (rows, 1, 1)]),
        in_specs=[SMEM, VMEM, ANY, ANY, ANY] + [VMEM] * len(arrived),
        out_specs=[VMEM] * 3,
        scratch_shapes=[
            pltpu.VMEM((rows, depth, pixels), jnp.float32),
            pltpu.VMEM((depth, pixels), jnp.float32),
            pltpu.VMEM(((rows + 2) * 3, pixels, pixels), jnp.float32),
            pltpu.VMEM((rows, pixels, pixels), jnp.float32),
            pltpu.VMEM((rows, depth // 3, pixels), jnp.float32),
        ]
        + fetch_scratch(fixed),
        compiler_params=pltpu.CompilerParams(
            vmem_limit_bytes=GRANT + sum(2 * part.size for part in arrived)
        ),
        cost_estimate=cost_of(9 * rows, pixels, depth, arrived),
        name="add_set",
    )(codes, note, *fixed, *arrived)


def add_ends(t, codes, note, left, weight, edge, *arrived):
    rows, pixels, depth = left.shape
    channels = depth // 3
    fixed = [keep(left), keep(weight), keep(edge)]
    shapes = [(1, DISP, pixels)] * 2
    shapes += [(2, depth, pixels), (2, pixels, pixels), (rows - 2, channels, pixels)]
    return pl.pallas_call(
        functools.partial(ends_kernel, t),
        out_shape=float_shapes(shapes),
        in_specs=[SMEM, VMEM, ANY, ANY, ANY] + [VMEM] * len(arrived),
        out_specs=[VMEM] * 5,
        scratch_shapes=[
            pltpu.VMEM((depth, pixels), jnp.float32),
            pltpu.VMEM(((rows + 2) * 3, pixels, pixels), jnp.float32),
            pltpu.VMEM((rows, channels, pixels), jnp.float32),
        ]
        + fetch_scratch(fixed),
        compiler_params=pltpu.CompilerParams(
            vmem_limit_bytes=GRANT + sum(2 * part.size for part in arrived)
        ),
        cost_estimate=cost_of(6, pixels, depth, arrived),
        name="add_ends",
    )(codes, note, *fixed, *arrived)


def add_middle(ends, left, weight, edge):
    rows, pixels, depth = left.shape
    return pl.pallas_call(
        middle_kernel,
        out_shape=float_shapes([(rows, DISP, pixels)])[0],
        in_specs=[VMEM] * 6,
        out_specs=VMEM,
        scratch_shapes=[
            pltpu.VMEM((rows - 2, depth, pixels), jnp.float32),
            pltpu.VMEM((depth, pixels), jnp.float32),
            pltpu.VMEM(((rows + 2) * 3, pixels, pixels), jnp.float32),
            pltpu.VMEM((rows - 2, pixels, pixels), jnp.float32),
        ],
        compiler_params=pltpu.CompilerParams(vmem_limit_bytes=14 << 20),
        cost_estimate=cost_of(9 * rows - 6, pixels, depth, ends),
        name="add_middle",
    )(*ends, left, weight, edge)


def depth_kernel(own_ref, far_ref, before_ref, before_far_ref, after_ref, after_far_ref, out_ref):
    rows, pixels = out_ref.shape
    level = (DISP - 1) - lax.broadcasted_iota(jnp.int32, (DISP, pixels), 0)
    share = level.astype(jnp.float32) / DISP
    depths = []
    for r in range(rows):
        scores = own_ref[r] + far_ref[r]
        if r == 0:
            scores = scores + (before_ref[0] + before_far_ref[0])
        if r == rows - 1:
            scores = scores + (after_ref[0] + after_far_ref[0])
        weights = jnp.exp(scores - jnp.max(scores, axis=0, keepdims=True))
        bottom = jnp.sum(weights, axis=0, keepdims=True)
        depths.append(jnp.sum(weights * share, axis=0, keepdims=True) / bottom)
    lane = lax.broadcasted_iota(jnp.int32, (8, pixels), 1)
    depth = jnp.concatenate(depths + [depths[0]] * (-rows % 8), axis=0)
    out_ref[...] = jnp.take_along_axis(depth, pixels - 1 - lane, axis=1)[:rows]


def depth_rows(*parts):
    rows, _, pixels = parts[0].shape
    return pl.pallas_call(
        depth_kernel,
        out_shape=jax.ShapeDtypeStruct((rows, pixels), jnp.float32),
        in_specs=[VMEM] * len(parts),
        out_specs=VMEM,
        compiler_params=pltpu.CompilerParams(vmem_limit_bytes=4 << 20),
        name="depth_rows",
    )(*parts)


def compute(source_rows, route_owner, target_row, start_index, reference_rows, conv_weight):
    views = lax.axis_size("views")
    half = views // 2
    _, channels, pixels = reference_rows.shape
    send = functools.partial(lax.ppermute, axis_name="views")
    home = [(i, (i + half) % views) for i in range(views)]
    groups = [list(range(half)), list(range(half, views))]
    swap = functools.partial(
        lax.all_to_all,
        axis_name="views",
        split_axis=0,
        concat_axis=0,
        tiled=True,
        axis_index_groups=groups,
    )
    owner = route_owner[:, 0]
    rest = target_row * DSPAN + start_index
    named = jnp.stack([owner, rest]).astype(jnp.bfloat16)
    named = jnp.pad(named, ((0, 0), (0, pixels - named.shape[1])), constant_values=-1)
    far_named = send(named, perm=home)
    far_rows = send(reference_rows, perm=home)
    apart = half <= 8
    *packed, slots = pack_rows(
        owner, target_row, start_index, source_rows, half, apart
    )
    count = len(packed) // SETS
    packed_far = list(add_note(packed[:count], slots, named, far_named))
    packed_own = list(packed[count:])

    def swap_all(parts):
        if not apart:
            return [swap(parts[0])]
        arrived = parts[:1] + [None] * (half - 1)
        for k in sorted(range(1, half), key=lambda k: (k < half // 2, -k % 2, -k)):
            arrived[k] = send(parts[k], perm=[(i, i ^ k) for i in range(views)])
        return arrived

    arrived_far = swap_all(packed_far)
    arrived_own = swap_all(packed_own)
    if apart:
        note = jnp.stack([part[CAP * channels :] for part in arrived_far])
    else:
        note = arrived_far[0][:, CAP * channels :]
    codes = note[:, 4, : SETS * CAP].astype(jnp.int32).reshape(-1)

    scaled = jnp.repeat(conv_weight / CG, CG, axis=0)
    taps = scaled.transpose(3, 0, 1, 2).reshape(-1, 9)
    taps = jnp.pad(taps, ((0, 0), (0, pixels - 9)))
    edges = jnp.pad(scaled[..., 2], ((0, 0), (0, 0), (0, 5))).reshape(-1, 24)
    edges = jnp.roll(jnp.pad(edges, ((0, 0), (0, pixels - 24))), -2, 1)
    near, far = stack_left(keep(reference_rows)), stack_left(far_rows)
    far_main, far_low, far_high = add_set(1, codes, note, far, taps, edges, *arrived_far)
    other_main = send(far_main, perm=home)
    other_low = send(far_low, perm=[(i, j - 1) for i, j in home if j > 0])
    other_high = send(far_high, perm=[(i, j + 1) for i, j in home if j + 1 < views])
    own_low, own_high, *ends = add_ends(0, codes, note, near, taps, edges, *arrived_own)
    own_low = send(own_low, perm=[(i, i - 1) for i in range(1, views)])
    own_high = send(own_high, perm=[(i, i + 1) for i in range(views - 1)])
    own_main = add_middle(ends, near, taps, edges)
    return depth_rows(own_main, other_main, own_high, other_high, own_low, other_low)


def solution(mesh):
    in_specs = (
        P(("groups", "views"), None, None),
        P(("groups", "views"), None),
        P(("groups", "views")),
        P(("groups", "views")),
        P(("groups", "views"), None, None),
        P(),
    )
    out_specs = P(("groups", "views"), None)
    return jax.shard_map(compute, mesh=mesh, in_specs=in_specs, out_specs=out_specs, check_vma=False)
```
